128 devices in a mesh: samp: 8 (over z_hi, y), chrom: 16 (over x, z_lo, core).
Axes of the slice: x: 4, y: 4, z: 4 (z_hi: 2, z_lo: 2; z = z_hi * 2 + z_lo), core: 2. Of those that a mesh axis runs over, the one named last changes fastest.
Arguments:
- dosages: float32 [8192, 16384], P('samp', 'chrom'), may hold values from -12 to 12
- traits: float32 [8192, 128], P('samp'), may hold values from -14 to 14
- start_coef: float32 [16384, 128], P('chrom'), may hold values from -1 to 1
- groups: int32 [16384], P('chrom'), may hold values from 0 to 31, as said below
- tested: bfloat16 [8192, 16384], P('samp', 'chrom'), may hold values from -16 to 16
- owners: int32 [16384], P('chrom'), may hold values from 0 to 31, as said below
Outputs:
- scores: float32 [16384, 128], P('chrom')
- residual: float32 [8192, 128], P('samp')
The draws below stay inside these ranges and needn't reach their ends.
Inputs may be any that keep to these rules, and one draw needn't show every extreme that they name: `groups`: training variant j belongs to group 2 * (j // 1024) + r with r from 0 to 1; every such group has a variant. `owners`: tested variant i belongs to group 2 * (i // 1024) + r with r from 0 to 1; every such group has a tested variant.
All inputs are finite; a program needn't handle non-finite values.
Results may differ from the reference program's by a relative error of at most 0.00045.
The reference program's roundings to bfloat16 on the way count: a program that leaves them out, or rounds other values in their place, can miss the bound.
Values sent between devices are 32-bit elements; how exact they have to be, the bound alone decides.
A program may use at most 64 MiB of HBM per device.

```python
import math
import jax
import jax.numpy as jnp
from jax import lax

M_DEV = 1024
K = 128
TEST_DEV = 1024
GPD = 2
ITERS = 2
N = 8192
M = 16384
TESTS = 16384
N_CHROM = 16


def strong_rows(key):
    phase = jax.random.randint(jax.random.fold_in(key, 31), (), 0, 2, dtype=jnp.int32)
    rows = jnp.arange(N, dtype=jnp.int32)
    return (rows % 2 == phase).astype(jnp.float32)[:, None]


def draw_dosages(key, part):
    strong = strong_rows(key)
    spread = jnp.exp(jax.random.uniform(jax.random.fold_in(key, 41), (N, 1), jnp.float32, 0.0, math.log(4.0)))
    base = jnp.clip(jax.random.normal(jax.random.fold_in(key, 43), (N, M), jnp.float32), -4.0, 4.0)
    return base * (0.5 * (1.0 + 0.4 * strong) * spread)


def draw_traits(key, part):
    rows = jnp.arange(N, dtype=jnp.float32) / N
    level = jnp.sqrt(0.5 + 4.0 * rows)[:, None]
    strong = strong_rows(key)
    col_phase = jax.random.randint(jax.random.fold_in(key, 33), (), 0, 2, dtype=jnp.int32)
    tied = (jnp.arange(K, dtype=jnp.int32) % 2 == col_phase).astype(jnp.float32)[None, :]
    agree = strong * tied + (1.0 - strong) * (1.0 - tied)
    factor = 0.625 + 0.975 * agree
    base = jnp.clip(jax.random.normal(jax.random.fold_in(key, 35), (N, K), jnp.float32), -4.0, 4.0)
    return base * level * factor


def draw_start_coef(key, part):
    scale = jnp.exp(jax.random.uniform(jax.random.fold_in(key, 3), (M, 1), jnp.float32, jnp.log(0.3), jnp.log(3.0)))
    base = jnp.clip(jax.random.normal(jax.random.fold_in(key, 51), (M, K), jnp.float32), -5.0, 5.0)
    return base * scale / jnp.sqrt(jnp.float32(M))


def draw_tested(key, part):
    rows = jnp.arange(N, dtype=jnp.float32) / N
    level = jnp.sqrt(1.0 + 8.0 * rows)[:, None]
    base = jnp.clip(jax.random.normal(jax.random.fold_in(key, 53), (N, TESTS), jnp.float32), -5.0, 5.0)
    return (base * level).astype(jnp.bfloat16)


def owned_groups(key, count, per_dev):
    index = jnp.arange(count, dtype=jnp.int32)
    block = index // per_dev
    place = index % per_dev
    pick = jax.random.randint(key, (count,), 0, GPD, dtype=jnp.int32)
    pick = jnp.where(place == 0, 0, jnp.where(place == per_dev - 1, GPD - 1, pick))
    return (block * GPD + pick).astype(jnp.int32)


def draw_groups(key, part):
    return owned_groups(jax.random.fold_in(key, 11), M, M_DEV)


def draw_owners(key, part):
    return owned_groups(jax.random.fold_in(key, 13), TESTS, TEST_DEV)


def setup_inputs(seed: int = 0) -> dict:
    arg_keys = jax.random.split(jax.random.key(seed), 7)
    dosages = draw_dosages(jax.random.fold_in(arg_keys[6], 71), 0)
    traits = draw_traits(jax.random.fold_in(arg_keys[6], 71), 0)
    start_coef = draw_start_coef(jax.random.fold_in(arg_keys[6], 71), 0)
    groups = draw_groups(jax.random.fold_in(arg_keys[6], 71), 0)
    tested = draw_tested(jax.random.fold_in(arg_keys[6], 71), 0)
    owners = draw_owners(jax.random.fold_in(arg_keys[6], 71), 0)
    return dict(dosages=dosages, traits=traits, start_coef=start_coef, groups=groups, tested=tested, owners=owners)


def matmul(left, right):
    return jnp.dot(left, right, precision=lax.Precision.HIGHEST, preferred_element_type=jnp.float32)

def inner_rows(left, right):
    return lax.dot_general(left, right, (((0,), (0,)), ((), ())), precision=lax.Precision.HIGHEST, preferred_element_type=jnp.float32)

def reference(dosages, traits, start_coef, groups, tested, owners):
    total_rows = dosages.shape[0]
    penalty = 1.5 * math.sqrt(traits.shape[1] / total_rows)
    coefficients = start_coef
    for iteration in range(ITERS):
        residual_now = traits - matmul(dosages, coefficients)
        gradient = inner_rows(dosages, residual_now) / total_rows
        image = matmul(dosages, gradient)
        grad_sq = jnp.sum(gradient * gradient)
        image_sq = jnp.sum(image * image)
        step_size = grad_sq / (image_sq / total_rows + 1e-06)
        moved_rows = coefficients + step_size * gradient
        length = jnp.sqrt(lax.optimization_barrier(jnp.sum(moved_rows * moved_rows, axis=1, keepdims=True)))
        coefficients = moved_rows * (jnp.maximum(length - step_size * penalty, 0.0) / jnp.maximum(length, step_size * penalty))
    residual = traits - matmul(dosages, coefficients)

    def score_block(block):
        start = (block * M_DEV).astype(jnp.int32)
        dos_block = lax.dynamic_slice_in_dim(dosages, start, M_DEV, 1)
        coef_block = lax.dynamic_slice_in_dim(coefficients, start, M_DEV, 0)
        group_block = lax.dynamic_slice_in_dim(groups, start, M_DEV, 0)
        test_start = (block * TEST_DEV).astype(jnp.int32)
        test_block = lax.dynamic_slice_in_dim(tested, test_start, TEST_DEV, 1)
        owner_block = lax.dynamic_slice_in_dim(owners, test_start, TEST_DEV, 0)
        group_base = (block * GPD).astype(jnp.int32)
        picked = jnp.zeros((TEST_DEV, traits.shape[1]), jnp.float32)
        loco_pick = jnp.zeros((TEST_DEV, traits.shape[1]), jnp.float32)
        for which in range(GPD):
            mask = (group_block - group_base == which).astype(jnp.float32)[:, None]
            own_part = matmul(dos_block, coef_block * mask)
            loco_resid = residual + own_part
            loco_sq = lax.optimization_barrier(jnp.sum(loco_resid * loco_resid, axis=0))
            products = lax.dot_general(test_block, loco_resid.astype(jnp.bfloat16), (((0,), (0,)), ((), ())), preferred_element_type=jnp.float32)
            chosen = (owner_block - group_base == which).astype(jnp.float32)[:, None]
            picked = picked + chosen * products
            loco_pick = loco_pick + chosen * loco_sq[None, :]
        tested_sq = lax.optimization_barrier(jnp.sum(jnp.square(test_block.astype(jnp.float32)), axis=0))
        denom = math.sqrt(total_rows) * jnp.sqrt((tested_sq[:, None] / total_rows + 1e-06) * (loco_pick / total_rows + 1e-06))
        return picked / denom
    scores = lax.map(score_block, jnp.arange(N_CHROM, dtype=jnp.int32))
    scores = scores.reshape((TESTS, traits.shape[1]))
    return (scores, residual)
```

```python
import math

import jax
import jax.numpy as jnp
from jax import lax
from jax.experimental import pallas as pl
from jax.experimental.pallas import tpu as pltpu
from jax.sharding import PartitionSpec as P

MESH = pl.DeviceIdType.MESH
F32 = jnp.float32
BF16 = jnp.bfloat16
ITERS = 2
ROWS = 1024
K = 128
N = 8192
PENALTY = 1.5 * math.sqrt(K / N)


def remote(src, dst, send_sem, recv_sem, dev):
    return pltpu.make_async_remote_copy(
        src_ref=src, dst_ref=dst, send_sem=send_sem, recv_sem=recv_sem, device_id=dev, device_id_type=MESH
    )


def wait_bytes(ref, sem):
    pltpu.make_async_copy(ref, ref, sem).wait()


def split(value):
    high = value.astype(BF16)
    low = (value - high.astype(F32)).astype(BF16)
    return high, low


def kernel(
    dos_hbm, traits_hbm, coef_hbm, groups_ref, tested_hbm, owners_ref,
    scores_ref, resid_ref,
    dos, traits, coef, tested, ds, dts, tts, weights, loco_w,
    part, coresum, corebuf, crecv, rfull, gpart, grecv, gfull,
    own0, own1, gmask, omask, tsq, tsq_recv, lsq, lsq_recv, scal,
    load_sem, core_send, core_recv, crs_send, crs_recv, cag_send, cag_recv, fwd_send, fwd_recv,
    srs_send, srs_recv, sag_send, sag_recv, scal_send, scal_recv, small_send, small_recv,
):
    s = lax.axis_index("samp")
    c = lax.axis_index("chrom")
    core = c % 2
    other = 1 - core
    q = c // 2
    x = q // 2
    z = q % 2
    me = s * 16 + c
    partner = (s, q * 2 + other)

    order = [(other, 1 - x // 2), (other, x // 2), (core, 1 - x // 2), (core, x // 2)]
    load_coef = pltpu.make_async_copy(coef_hbm, coef, load_sem.at[0])
    load_coef.start()
    load_dos = []
    for i, (half, far) in enumerate(order):
        rows = pl.ds((half * 2 + far) * 256, 256)
        cp = pltpu.make_async_copy(dos_hbm.at[rows], dos.at[rows], load_sem.at[1 + i])
        cp.start()
        load_dos.append(cp)
    load_traits = pltpu.make_async_copy(traits_hbm, traits, load_sem.at[5])
    load_traits.start()
    load_tested = pltpu.make_async_copy(tested_hbm, tested, load_sem.at[6])
    load_tested.start()

    bar = pltpu.get_barrier_semaphore()

    @pl.loop(1, 128)
    def _(k):
        t = (me + k) % 128
        pl.semaphore_signal(bar, inc=1, device_id=(t // 16, t % 16), device_id_type=MESH)

    def set_weights(value, at=0):
        high, low = split(value)
        weights[:, at:at + K] = high
        weights[:, at + K:at + 2 * K] = low

    def chunk_dot(lhs, chunk, rhs):
        out = jnp.dot(lhs[chunk], rhs, preferred_element_type=F32)
        return (out[:256, :K] + (out[:256, K:] + out[256:, K:])) + out[256:, :K]

    def chrom_rs(ph, compute, filler=None):
        for i, (half, far) in enumerate(order):
            chunk = half * 2 + far
            value = compute(i, chunk)
            if i < 2:
                part[ph, i] = value
                remote(part.at[ph, i], corebuf.at[ph, i], core_send.at[ph, i], core_recv.at[ph, i], partner).start()
            else:
                part[ph, i] = value
        for i in range(2):
            far = order[i][1]
            wait_bytes(corebuf.at[ph, i], core_recv.at[ph, i])
            coresum[ph, pl.ds(far * 256, 256), :] = part[ph, 2 + i] + corebuf[ph, i]
            for j in range(4):
                t = far * 4 + j

                @pl.when(t != q)
                def _():
                    remote(
                        coresum.at[ph, pl.ds(t * 64, 64)], crecv.at[ph, q],
                        crs_send.at[ph], crs_recv.at[ph], (s, t * 2 + core),
                    ).start()
        crecv[ph, q] = coresum[ph, pl.ds(pl.multiple_of(q * 64, 64), 64), :]
        if filler is not None:
            filler()
        wait_bytes(crecv.at[ph, pl.ds(0, 7)], crs_recv.at[ph])
        total = crecv[ph, 0]
        for k in range(1, 8):
            total = total + crecv[ph, k]
        return total

    near = [(0, 1), (1, 0), (3, 0), (1, 1), (3, 1), (2, 0), (2, 1)]

    def chrom_ag(a, full, filler=None):
        base = core * 512
        mine = pl.ds(pl.multiple_of(base + q * 64, 64), 64)
        for dx, dz in reversed(near):
            t = (x + dx) % 4 * 2 + (z + dz) % 2
            remote(full.at[mine], full.at[mine], cag_send.at[a], cag_recv.at[a, q], (s, t * 2 + core)).start()
        remote(full.at[mine], full.at[mine], fwd_send.at[a], fwd_recv.at[a], partner).start()
        if filler is not None:
            filler()
        for dx, dz in near:
            t = (x + dx) % 4 * 2 + (z + dz) % 2
            rows = pl.ds(pl.multiple_of(base + t * 64, 64), 64)
            wait_bytes(full.at[rows], cag_recv.at[a, t])
            remote(full.at[rows], full.at[rows], fwd_send.at[a], fwd_recv.at[a], partner).start()
        wait_bytes(full.at[pl.ds(0, 512)], fwd_recv.at[a])

    def samp_rs(ph, compute, filler=None):
        for j in range(4):
            chunk = (s // 2 + 1 + j) % 4
            gpart[ph, pl.ds(pl.multiple_of(chunk * 256, 256), 256), :] = compute(chunk)
            for k in range(2):
                t = chunk * 2 + k

                @pl.when(t != s)
                def _():
                    remote(
                        gpart.at[ph, pl.ds(t * 128, 128)], grecv.at[ph, s],
                        srs_send.at[ph], srs_recv.at[ph], (t, c),
                    ).start()
        grecv[ph, s] = gpart[ph, pl.ds(pl.multiple_of(s * 128, 128), 128), :]
        if filler is not None:
            filler()
        wait_bytes(grecv.at[ph, pl.ds(0, 7)], srs_recv.at[ph])
        total = grecv[ph, 0]
        for k in range(1, 8):
            total = total + grecv[ph, k]
        return total

    def samp_ag(ph, full, filler=None):
        mine = pl.ds(pl.multiple_of(s * 128, 128), 128)
        for k in (6, 2, 5, 7, 3, 1, 4):
            t = (s // 4 + k // 4) % 2 * 4 + (s + k) % 4
            remote(full.at[mine], full.at[mine], sag_send.at[ph], sag_recv.at[ph], (t, c)).start()
        if filler is not None:
            filler()
        wait_bytes(full.at[pl.ds(0, 896)], sag_recv.at[ph])

    def prepare_transposed():
        @pl.loop(0, 16)
        def _(b):
            i, j = b // 4, b % 4
            rows = pl.ds(pl.multiple_of(i * 256, 256), 256)
            cols = pl.ds(pl.multiple_of(j * 256, 256), 256)
            high, low = split(dos[rows, cols].T)
            dts[j, 0:256, rows] = high
            dts[j, 256:512, rows] = low

    def prepare_tested():
        load_tested.wait()

        @pl.loop(0, 16)
        def _(b):
            i, j = b // 4, b % 4
            rows = pl.ds(pl.multiple_of(i * 256, 256), 256)
            cols = pl.ds(pl.multiple_of(j * 256, 256), 256)
            tts[j, :, rows] = tested[rows, cols].astype(F32).T.astype(BF16)

    def prepare_masks():
        for b in range(8):
            rows = slice(b * 128, b * 128 + 128)
            g = (groups_ref[b:b + 1, :] - c * 2).astype(F32)
            gmask[rows, :] = jnp.broadcast_to(g, (128, 128)).T
            o = (owners_ref[b:b + 1, :] - c * 2).astype(F32)
            omask[rows, :] = jnp.broadcast_to(o, (128, 128)).T

    def prepare_tsq():
        for b in range(8):
            def add(i, acc):
                value = tested[pl.ds(pl.multiple_of(i * 128, 128), 128), b * 128:(b + 1) * 128].astype(F32)
                return acc + jnp.sum((value * value).reshape(16, 8, 128), axis=0)
            acc = lax.fori_loop(0, 8, add, jnp.zeros((8, 128), F32))
            tsq[b:b + 1, :] = jnp.sum(acc, axis=0, keepdims=True)
        for k in range(1, 8):
            t = (s + k) % 8
            remote(tsq.at[pl.ds(t, 1)], tsq_recv.at[pl.ds(s, 1)], small_send.at[0], small_recv.at[0], (t, c)).start()
        tsq_recv[pl.ds(s, 1), :] = tsq[pl.ds(s, 1), :]

    load_coef.wait()
    set_weights(coef[...])

    def split_chunk(i, chunk):
        load_dos[i].wait()
        high, low = split(dos[pl.ds(pl.multiple_of(chunk * 256, 256), 256), :])
        ds[chunk, 0:256, :] = high
        ds[chunk, 256:512, :] = low

    def first_compute(i, chunk):
        split_chunk(i, chunk)
        if i == 0:
            pl.semaphore_wait(bar, 127)
        return chunk_dot(ds, chunk, weights[:, 0:256])

    def plain_compute(i, chunk):
        return chunk_dot(ds, chunk, weights[:, 0:256])

    lane = lax.broadcasted_iota(jnp.int32, (1, K), 1)
    shard64 = pl.ds(pl.multiple_of(core * 512 + q * 64, 64), 64)
    shard128 = pl.ds(pl.multiple_of(s * 128, 128), 128)

    for it in range(ITERS):
        total = chrom_rs(2 * it, first_compute if it == 0 else plain_compute,
                         prepare_transposed if it == 0 else None)
        if it == 0:
            load_traits.wait()
        rfull[it, shard64, :] = traits[shard64, :] - total
        chrom_ag(it, rfull.at[it])
        high, low = split(rfull[it])
        weights[:, 0:K] = high
        weights[:, K:2 * K] = low
        total = samp_rs(it, lambda chunk: chunk_dot(dts, chunk, weights[:, 0:256]),
                        prepare_masks if it == 1 else None)
        grad = total * (1.0 / N)
        gfull[it, shard128, :] = grad
        samp_ag(it, gfull.at[it], prepare_tested if it == 0 else prepare_tsq)
        set_weights(gfull[it])
        image = chrom_rs(2 * it + 1, plain_compute)
        g_row = jnp.sum(grad * grad, axis=0, keepdims=True)
        i_row = jnp.sum(image * image, axis=0, keepdims=True)
        g_row = g_row + pltpu.roll(g_row, 64, 1)
        i_row = i_row + pltpu.roll(i_row, 64, 1)
        scal[it, pl.ds(me, 1), :] = jnp.where(lane < 64, g_row, i_row)

        @pl.loop(1, 128)
        def _(k):
            t = (me + 128 - k) % 128
            remote(scal.at[it, pl.ds(me, 1)], scal.at[it, pl.ds(me, 1)], scal_send.at[it], scal_recv.at[it],
                   (t // 16, t % 16)).start()
        wait_bytes(scal.at[it, pl.ds(0, 127)], scal_recv.at[it])
        sums = jnp.sum(scal[it], axis=0, keepdims=True)
        grad_sq = jnp.sum(jnp.where(lane < 64, sums, 0.0), axis=1, keepdims=True)
        image_sq = jnp.sum(jnp.where(lane < 64, 0.0, sums), axis=1, keepdims=True)
        step = grad_sq / (image_sq * (1.0 / N) + 1e-06)
        moved = coef[...] + step * gfull[it]
        length = jnp.sqrt(jnp.sum(moved * moved, axis=1, keepdims=True))
        limit = step * PENALTY
        new = moved * (jnp.maximum(length - limit, 0.0) / jnp.maximum(length, limit))
        if it + 1 < ITERS:
            coef[...] = new
            set_weights(new)
        else:
            set_weights(new * (1.0 - gmask[...]), 0)
            set_weights(new * gmask[...], 256)

    def final_compute(i, chunk):
        rows = pl.ds(pl.multiple_of(chunk * 256, 256), 256)
        a = chunk_dot(ds, chunk, weights[:, 0:256])
        b = chunk_dot(ds, chunk, weights[:, 256:512])
        own0[rows, :] = a
        own1[rows, :] = b
        return a + b

    total = chrom_rs(4, final_compute)
    resid_ref[shard64, :] = traits[shard64, :] - total
    chrom_ag(2, resid_ref)
    res = resid_ref[...]
    loco0 = res + own0[...]
    loco1 = res + own1[...]
    lsq[0:1, :] = jnp.sum(loco0 * loco0, axis=0, keepdims=True)
    lsq[1:2, :] = jnp.sum(loco1 * loco1, axis=0, keepdims=True)
    loco_w[:, 0:K] = loco0.astype(BF16)
    loco_w[:, K:2 * K] = loco1.astype(BF16)
    for k in range(1, 8):
        t = (s + k) % 8
        remote(lsq, lsq_recv.at[s], small_send.at[1], small_recv.at[1], (t, c)).start()
    lsq_recv[s] = lsq[...]

    def products(chunk):
        out = jnp.dot(tts[chunk], loco_w[...], preferred_element_type=F32)
        which = omask[pl.ds(pl.multiple_of(chunk * 256, 256), 256), :]
        return jnp.where(which < 0.5, out[:, :K], out[:, K:])

    picked = samp_rs(2, products)
    wait_bytes(tsq_recv.at[pl.ds(0, 7)], small_recv.at[0])
    wait_bytes(lsq_recv.at[pl.ds(0, 7)], small_recv.at[1])
    tsum = jnp.sum(tsq_recv[...], axis=0, keepdims=True)
    tcol = jnp.broadcast_to(tsum, (128, 128)).T
    lsum = lsq_recv[0]
    for k in range(1, 8):
        lsum = lsum + lsq_recv[k]
    lpick = jnp.where(omask[shard128, :] < 0.5, lsum[0:1, :], lsum[1:2, :])
    denom = math.sqrt(N) * jnp.sqrt((tcol * (1.0 / N) + 1e-06) * (lpick * (1.0 / N) + 1e-06))
    scores_ref[shard128, :] = picked / denom
    samp_ag(2, scores_ref)

    for ph in range(5):
        for i in range(2):
            wait_bytes(corebuf.at[ph, i], core_send.at[ph, i])
        wait_bytes(crecv.at[ph, pl.ds(0, 7)], crs_send.at[ph])
    for a in range(3):
        wait_bytes(rfull.at[0, pl.ds(0, 448)], cag_send.at[a])
        wait_bytes(rfull.at[0, pl.ds(0, 512)], fwd_send.at[a])
        wait_bytes(grecv.at[a, pl.ds(0, 7)], srs_send.at[a])
        wait_bytes(gfull.at[0, pl.ds(0, 896)], sag_send.at[a])
    for it in range(ITERS):
        wait_bytes(scal.at[it, pl.ds(0, 127)], scal_send.at[it])
    wait_bytes(tsq_recv.at[pl.ds(0, 7)], small_send.at[0])
    wait_bytes(lsq_recv.at[pl.ds(0, 7)], small_send.at[1])


def body(dosages, traits, start_coef, groups, tested, owners):
    any_spec = pl.BlockSpec(memory_space=pl.ANY)
    vmem_spec = pl.BlockSpec(memory_space=pltpu.VMEM)
    V = pltpu.VMEM
    DMA = pltpu.SemaphoreType.DMA
    out = jax.ShapeDtypeStruct((ROWS, K), F32)
    return pl.pallas_call(
        kernel,
        out_shape=(out, out),
        in_specs=[any_spec, any_spec, any_spec, vmem_spec, any_spec, vmem_spec],
        out_specs=(vmem_spec, vmem_spec),
        scratch_shapes=[
            V((1024, 1024), F32), V((1024, K), F32), V((1024, K), F32), V((1024, 1024), BF16),
            V((4, 512, 1024), BF16), V((4, 512, 1024), BF16), V((4, 256, 1024), BF16),
            V((1024, 512), BF16), V((1024, 256), BF16),
            V((5, 4, 256, K), F32), V((5, 512, K), F32), V((5, 2, 256, K), F32), V((5, 8, 64, K), F32),
            V((2, 1024, K), F32), V((3, 1024, K), F32), V((3, 8, 128, K), F32), V((2, 1024, K), F32),
            V((1024, K), F32), V((1024, K), F32), V((1024, K), F32), V((1024, K), F32),
            V((8, K), F32), V((8, K), F32), V((2, K), F32), V((8, 2, K), F32), V((2, 128, K), F32),
            DMA((8,)), DMA((5, 2)), DMA((5, 2)), DMA((5,)), DMA((5,)), DMA((3,)), DMA((3, 8)), DMA((3,)), DMA((3,)),
            DMA((3,)), DMA((3,)), DMA((3,)), DMA((3,)), DMA((2,)), DMA((2,)), DMA((2,)), DMA((2,)),
        ],
        compiler_params=pltpu.CompilerParams(
            collective_id=0, has_side_effects=True, vmem_limit_bytes=60 * 1024 * 1024
        ),
    )(dosages, traits, start_coef, groups.reshape(8, 128), tested, owners.reshape(8, 128))


def solution(mesh):
    placed = (P("samp", "chrom"), P("samp", None), P("chrom", None), P("chrom"), P("samp", "chrom"), P("chrom"))
    return jax.shard_map(
        body, mesh=mesh, in_specs=placed, out_specs=(P("chrom", None), P("samp", None)), check_vma=False
    )
```

```python
import math

import jax
import jax.numpy as jnp
from jax import lax
from jax.experimental import pallas as pl
from jax.experimental.pallas import tpu as pltpu
from jax.sharding import PartitionSpec as P

MESH = pl.DeviceIdType.MESH
F32 = jnp.float32
BF16 = jnp.bfloat16
ITERS = 2
ROWS = 1024
K = 128
N = 8192
PENALTY = 1.5 * math.sqrt(K / N)


def remote(src, dst, send_sem, recv_sem, dev):
    return pltpu.make_async_remote_copy(
        src_ref=src, dst_ref=dst, send_sem=send_sem, recv_sem=recv_sem, device_id=dev, device_id_type=MESH
    )


def wait_bytes(ref, sem):
    pltpu.make_async_copy(ref, ref, sem).wait()


def split(value):
    high = value.astype(BF16)
    low = (value - high.astype(F32)).astype(BF16)
    return high, low


def kernel(
    dos_hbm, traits_hbm, coef_hbm, groups_ref, tested_hbm, owners_ref,
    scores_out, resid_out,
    dos, traits, coef, tested, ds, dts, tts, weights, loco_w,
    part, coresum, corebuf, crecv, rfull, gpart, grecv, gfull, score,
    own0, own1, gmask, omask, tcol, tsq_recv, lsq_recv, scal,
    load_sem, core_send, core_recv, far_send, crs_send, crs_recv, cag_send, cag_recv, fwd_send, fwd_recv,
    far_recv, srs_send, srs_recv, sag_send, sag_recv, scal_send, scal_recv, small_send, small_recv, out_sem,
):
    s = lax.axis_index("samp")
    c = lax.axis_index("chrom")
    core = c % 2
    other = 1 - core
    q = c // 2
    x = q // 2
    z = q % 2
    me = s * 16 + c
    partner = (s, q * 2 + other)
    opposite = (x + 2) % 4 * 2 + (1 - z)

    def chip(dx, dz):
        return (x + dx) % 4 * 2 + (z + dz) % 2

    def samp_peer(k):
        return (s // 4 + k // 4) % 2 * 4 + (s + k) % 4

    far_first = [(2, 0), (1, 1), (3, 1), (1, 0), (3, 0), (0, 1)]
    samp_order = (6, 2, 5, 7, 3, 1, 4)

    bar = pltpu.get_barrier_semaphore()
    for k in samp_order:
        pl.semaphore_signal(bar, inc=1, device_id=(samp_peer(k), c), device_id_type=MESH)
    for dx, dz in [(2, 1)] + far_first:
        pl.semaphore_signal(bar, inc=1, device_id=(s, chip(dx, dz) * 2 + core), device_id_type=MESH)
    pl.semaphore_signal(bar, inc=1, device_id=(s, opposite * 2 + other), device_id_type=MESH)
    pl.semaphore_signal(bar, inc=1, device_id=partner, device_id_type=MESH)

    order = [other * 2, other * 2 + 1, core * 2, core * 2 + 1]
    load_coef = pltpu.make_async_copy(coef_hbm, coef, load_sem.at[0])
    load_coef.start()
    load_dos = []
    for i, chunk in enumerate(order):
        rows = pl.ds(pl.multiple_of(chunk * 256, 256), 256)
        cp = pltpu.make_async_copy(dos_hbm.at[rows], dos.at[rows], load_sem.at[1 + i])
        cp.start()
        load_dos.append(cp)
    load_traits = pltpu.make_async_copy(traits_hbm, traits, load_sem.at[5])
    load_traits.start()
    load_tested = pltpu.make_async_copy(tested_hbm, tested, load_sem.at[6])
    load_tested.start()

    def set_weights(block, value, at=0):
        rows = slice(block * 128, block * 128 + 128)
        high, low = split(value)
        weights[rows, at:at + K] = high
        weights[rows, at + K:at + 2 * K] = low

    def blocks(ref):
        return [ref[b * 128:b * 128 + 128, :] for b in range(8)]

    def chunk_dot(lhs, chunk, rhs):
        out = jnp.dot(lhs[chunk], rhs, preferred_element_type=F32)
        return (out[:256, :K] + (out[:256, K:] + out[256:, K:])) + out[256:, :K]

    def rows32(t, u, half):
        return pl.ds(pl.multiple_of(half * 512 + u * 256 + t * 32, 32), 32)

    def chrom_rs(ph, compute, done, filler=None):
        cut = pl.ds(pl.multiple_of(opposite * 32, 32), 32)
        mine = pl.ds(pl.multiple_of(q * 32, 32), 32)
        for i, chunk in enumerate(order):
            u = i % 2
            part[ph, i] = compute(i, chunk)
            if i < 2:
                remote(part.at[ph, i], corebuf.at[ph, u], core_send.at[ph, u], core_recv.at[ph, u], partner).start()
                remote(part.at[ph, i, cut], crecv.at[ph, u, 8], far_send.at[ph], crs_recv.at[ph, u],
                       (s, opposite * 2 + other)).start()
            else:
                remote(part.at[ph, i, cut], crecv.at[ph, u, q], far_send.at[ph], crs_recv.at[ph, u],
                       (s, opposite * 2 + core)).start()
        for u in range(2):
            wait_bytes(corebuf.at[ph, u], core_recv.at[ph, u])
            coresum[ph, u] = part[ph, 2 + u] + corebuf[ph, u]
            for dx, dz in far_first:
                t = chip(dx, dz)
                remote(coresum.at[ph, u, pl.ds(pl.multiple_of(t * 32, 32), 32)], crecv.at[ph, u, q],
                       crs_send.at[ph], crs_recv.at[ph, u], (s, t * 2 + core)).start()
            crecv[ph, u, q] = coresum[ph, u, mine, :]
        if filler is not None:
            filler()
        for u in range(2):
            wait_bytes(crecv.at[ph, u, pl.ds(0, 8)], crs_recv.at[ph, u])
            total = crecv[ph, u, 0]
            for k in range(1, 9):
                total = total + crecv[ph, u, k]
            done(u, total)

    def chrom_ag_send(a, full, u):
        mine = rows32(q, u, core)
        remote(full.at[mine], full.at[mine], cag_send.at[a], cag_recv.at[a, u, q],
               (s, opposite * 2 + core)).start()
        remote(full.at[mine], full.at[mine], cag_send.at[a], far_recv.at[a, u],
               (s, opposite * 2 + other)).start()
        for dx, dz in far_first:
            remote(full.at[mine], full.at[mine], cag_send.at[a], cag_recv.at[a, u, q],
                   (s, chip(dx, dz) * 2 + core)).start()
        remote(full.at[mine], full.at[mine], fwd_send.at[a], fwd_recv.at[a, u], partner).start()

    def chrom_ag_wait(a, full):
        for u in range(2):
            for dx, dz in reversed(far_first):
                t = chip(dx, dz)
                rows = rows32(t, u, core)
                wait_bytes(full.at[rows], cag_recv.at[a, u, t])
                remote(full.at[rows], full.at[rows], fwd_send.at[a], fwd_recv.at[a, u], partner).start()
        for u in range(2):
            wait_bytes(full.at[rows32(0, u, core)], cag_recv.at[a, u, opposite])
            wait_bytes(full.at[rows32(0, u, core)], far_recv.at[a, u])
            wait_bytes(full.at[pl.ds(0, 224)], fwd_recv.at[a, u])

    def srows(t, u):
        return pl.ds(pl.multiple_of(u * 256 + t * 32, 32), 32)

    def samp_rs(ph, compute, done, filler=None):
        for u in range(4):
            gpart[ph, u] = compute(u)
            for k in samp_order:
                t = samp_peer(k)
                remote(gpart.at[ph, u, pl.ds(pl.multiple_of(t * 32, 32), 32)], grecv.at[ph, u, s],
                       srs_send.at[ph], srs_recv.at[ph, u], (t, c)).start()
            grecv[ph, u, s] = gpart[ph, u, pl.ds(pl.multiple_of(s * 32, 32), 32), :]
        if filler is not None:
            filler()
        for u in range(4):
            wait_bytes(grecv.at[ph, u, pl.ds(0, 7)], srs_recv.at[ph, u])
            total = grecv[ph, u, 0]
            for k in range(1, 8):
                total = total + grecv[ph, u, k]
            done(u, total)

    def samp_ag_send(ph, src, dst, u):
        for k in samp_order:
            remote(src, dst, sag_send.at[ph], sag_recv.at[ph, u], (samp_peer(k), c)).start()

    def samp_ag_wait(ph, u):
        wait_bytes(gfull.at[0, pl.ds(0, 224)], sag_recv.at[ph, u])

    def prepare_transposed():
        @pl.loop(0, 16)
        def _(b):
            i, j = b // 4, b % 4
            rows = pl.ds(pl.multiple_of(i * 256, 256), 256)
            cols = pl.ds(pl.multiple_of(j * 256, 256), 256)
            high, low = split(dos[rows, cols].T)
            dts[j, 0:256, rows] = high
            dts[j, 256:512, rows] = low

    def prepare_tested():
        @pl.loop(0, 16)
        def _(b):
            i, j = b // 4, b % 4
            rows = pl.ds(pl.multiple_of(i * 256, 256), 256)
            cols = pl.ds(pl.multiple_of(j * 256, 256), 256)
            tts[j, :, rows] = tested[rows, cols].astype(F32).T.astype(BF16)

    def prepare_tsq():
        load_tested.wait()
        for b in range(8):
            def add(i, acc):
                value = tested[pl.ds(pl.multiple_of(i * 128, 128), 128), b * 128:(b + 1) * 128].astype(F32)
                return acc + jnp.sum((value * value).reshape(16, 8, 128), axis=0)
            acc = lax.fori_loop(0, 8, add, jnp.zeros((8, 128), F32))
            tsq_recv[s, pl.ds(b, 1), :] = jnp.sum(acc, axis=0, keepdims=True)
        for k in samp_order:
            remote(tsq_recv.at[s], tsq_recv.at[s], small_send.at[0], small_recv.at[0], (samp_peer(k), c)).start()

    def prepare_masks():
        for b in range(8):
            rows = slice(b * 128, b * 128 + 128)
            g = (groups_ref[b:b + 1, :] - c * 2).astype(F32)
            gmask[rows, :] = jnp.broadcast_to(g, (128, 128)).T
            o = (owners_ref[b:b + 1, :] - c * 2).astype(F32)
            omask[rows, :] = jnp.broadcast_to(o, (128, 128)).T

    def prepare_tcol():
        wait_bytes(tsq_recv.at[pl.ds(0, 7)], small_recv.at[0])
        total = tsq_recv[0]
        for k in range(1, 8):
            total = total + tsq_recv[k]
        for b in range(8):
            tcol[b * 128:b * 128 + 128, :] = jnp.broadcast_to(total[b:b + 1, :], (128, 128)).T

    load_coef.wait()
    for b, value in enumerate(blocks(coef)):
        set_weights(b, value)

    def first_compute(i, chunk):
        load_dos[i].wait()
        high, low = split(dos[pl.ds(pl.multiple_of(chunk * 256, 256), 256), :])
        ds[chunk, 0:256, :] = high
        ds[chunk, 256:512, :] = low
        value = chunk_dot(ds, chunk, weights[:, 0:256])
        if i == 0:
            pl.semaphore_wait(bar, 16)
        return value

    def plain_compute(i, chunk):
        return chunk_dot(ds, chunk, weights[:, 0:256])

    lane = lax.broadcasted_iota(jnp.int32, (1, K), 1)

    for it in range(ITERS):
        def residual_done(u, total):
            if it == 0 and u == 0:
                load_traits.wait()
            rows = rows32(q, u, core)
            rfull[it, rows, :] = traits[rows, :] - total
            chrom_ag_send(it, rfull.at[it], u)

        chrom_rs(2 * it, first_compute if it == 0 else plain_compute, residual_done,
                 prepare_transposed if it == 0 else prepare_tcol)
        chrom_ag_wait(it, rfull.at[it])
        for b, value in enumerate(blocks(rfull.at[it])):
            set_weights(b, value)

        squares = []

        def gradient_done(u, total):
            grad = total * (1.0 / N)
            squares.append(jnp.sum(grad * grad, axis=0, keepdims=True))
            gfull[it, srows(s, u), :] = grad
            samp_ag_send(it, gfull.at[it, srows(s, u)], gfull.at[it, srows(s, u)], u)

        samp_rs(it, lambda u: chunk_dot(dts, u, weights[:, 0:256]), gradient_done,
                prepare_tsq if it == 0 else prepare_masks)
        if it == 0:
            prepare_tested()
        for u in range(4):
            samp_ag_wait(it, u)
            for b in (2 * u, 2 * u + 1):
                set_weights(b, gfull[it, b * 128:b * 128 + 128, :])
        g_row = (squares[0] + squares[1]) + (squares[2] + squares[3])
        g_row = g_row + pltpu.roll(g_row, 64, 1)
        image_squares = []
        chrom_rs(2 * it + 1, plain_compute,
                 lambda u, total: image_squares.append(jnp.sum(total * total, axis=0, keepdims=True)))
        i_row = image_squares[0] + image_squares[1]
        i_row = i_row + pltpu.roll(i_row, 64, 1)
        scal[it, pl.ds(me, 1), :] = jnp.where(lane < 64, g_row, i_row)

        @pl.loop(1, 128)
        def _(k):
            t = (me + 128 - k) % 128
            remote(scal.at[it, pl.ds(me, 1)], scal.at[it, pl.ds(me, 1)], scal_send.at[it], scal_recv.at[it],
                   (t // 16, t % 16)).start()
        wait_bytes(scal.at[it, pl.ds(0, 127)], scal_recv.at[it])
        sums = jnp.sum(scal[it], axis=0, keepdims=True)
        grad_sq = jnp.sum(jnp.where(lane < 64, sums, 0.0), axis=1, keepdims=True)
        image_sq = jnp.sum(jnp.where(lane < 64, 0.0, sums), axis=1, keepdims=True)
        step = grad_sq / (image_sq * (1.0 / N) + 1e-06)
        limit = step * PENALTY
        for b in range(8):
            rows = slice(b * 128, b * 128 + 128)
            moved = coef[rows, :] + step * gfull[it, rows, :]
            length = jnp.sqrt(jnp.sum(moved * moved, axis=1, keepdims=True))
            new = moved * (jnp.maximum(length - limit, 0.0) / jnp.maximum(length, limit))
            if it + 1 < ITERS:
                coef[rows, :] = new
                set_weights(b, new)
            else:
                second = new * gmask[rows, :]
                set_weights(b, new * (1.0 - gmask[rows, :]), 0)
                set_weights(b, second, 256)

    def final_compute(i, chunk):
        rows = pl.ds(pl.multiple_of(chunk * 256, 256), 256)
        a = chunk_dot(ds, chunk, weights[:, 0:256])
        b = chunk_dot(ds, chunk, weights[:, 256:512])
        own0[rows, :] = a
        own1[rows, :] = b
        return a + b

    def last_residual_done(u, total):
        rows = rows32(q, u, core)
        rfull[2, rows, :] = traits[rows, :] - total
        chrom_ag_send(2, rfull.at[2], u)

    chrom_rs(4, final_compute, last_residual_done)
    chrom_ag_wait(2, rfull.at[2])
    give_resid = pltpu.make_async_copy(rfull.at[2], resid_out, out_sem.at[0])
    give_resid.start()
    sq0 = jnp.zeros((1, K), F32)
    sq1 = jnp.zeros((1, K), F32)
    for b in range(8):
        rows = slice(b * 128, b * 128 + 128)
        res = rfull[2, rows, :]
        loco0 = res + own0[rows, :]
        loco1 = res + own1[rows, :]
        sq0 = sq0 + jnp.sum(loco0 * loco0, axis=0, keepdims=True)
        sq1 = sq1 + jnp.sum(loco1 * loco1, axis=0, keepdims=True)
        loco_w[rows, 0:K] = loco0.astype(BF16)
        loco_w[rows, K:2 * K] = loco1.astype(BF16)
    lsq_recv[s, 0:1, :] = sq0
    lsq_recv[s, 1:2, :] = sq1
    for k in samp_order:
        remote(lsq_recv.at[s], lsq_recv.at[s], small_send.at[1], small_recv.at[1], (samp_peer(k), c)).start()

    def products(u):
        out = jnp.dot(tts[u], loco_w[...], preferred_element_type=F32)
        return jnp.where(omask[u * 256:u * 256 + 256, :] < 0.5, out[:, :K], out[:, K:])

    def score_done(u, picked):
        if u == 0:
            wait_bytes(lsq_recv.at[pl.ds(0, 7)], small_recv.at[1])
        lsum = lsq_recv[0]
        for k in range(1, 8):
            lsum = lsum + lsq_recv[k]
        rows = srows(s, u)
        lpick = jnp.where(omask[rows, :] < 0.5, lsum[0:1, :], lsum[1:2, :])
        denom = math.sqrt(N) * jnp.sqrt((tcol[rows, :] * (1.0 / N) + 1e-06) * (lpick * (1.0 / N) + 1e-06))
        score[u] = picked / denom
        samp_ag_send(2, score.at[u], scores_out.at[rows], u)
        pltpu.make_async_copy(score.at[u], scores_out.at[rows], out_sem.at[1 + u]).start()

    samp_rs(2, products, score_done)
    for u in range(4):
        samp_ag_wait(2, u)
        wait_bytes(score.at[u], out_sem.at[1 + u])
    give_resid.wait()

    for ph in range(5):
        for u in range(2):
            wait_bytes(corebuf.at[ph, u], core_send.at[ph, u])
        wait_bytes(rfull.at[0, pl.ds(0, 128)], far_send.at[ph])
        wait_bytes(rfull.at[0, pl.ds(0, 384)], crs_send.at[ph])
    for a in range(3):
        wait_bytes(rfull.at[0, pl.ds(0, 512)], cag_send.at[a])
        wait_bytes(rfull.at[0, pl.ds(0, 448)], fwd_send.at[a])
        wait_bytes(rfull.at[0, pl.ds(0, 896)], srs_send.at[a])
        wait_bytes(rfull.at[0, pl.ds(0, 896)], sag_send.at[a])
    for it in range(ITERS):
        wait_bytes(scal.at[it, pl.ds(0, 127)], scal_send.at[it])
    wait_bytes(tsq_recv.at[pl.ds(0, 7)], small_send.at[0])
    wait_bytes(lsq_recv.at[pl.ds(0, 7)], small_send.at[1])


def hand_over_kernel(a_in, b_in, a_out, b_out, buf, in_sem, out_sem):
    pairs = [(a_in, a_out, i) for i in range(2)] + [(b_in, b_out, i) for i in range(2)]
    loads, stores = [], []
    for n, (src, _, i) in enumerate(pairs):
        loads.append(pltpu.make_async_copy(src.at[pl.ds(i * 512, 512)], buf.at[n], in_sem.at[n]))
        loads[-1].start()
    for n, (_, dst, i) in enumerate(pairs):
        loads[n].wait()
        stores.append(pltpu.make_async_copy(buf.at[n], dst.at[pl.ds(i * 512, 512)], out_sem.at[n]))
        stores[-1].start()
    for cp in stores:
        cp.wait()


def body(dosages, traits, start_coef, groups, tested, owners):
    any_spec = pl.BlockSpec(memory_space=pl.ANY)
    vmem_spec = pl.BlockSpec(memory_space=pltpu.VMEM)
    V = pltpu.VMEM
    DMA = pltpu.SemaphoreType.DMA
    out = jax.ShapeDtypeStruct((ROWS, K), F32)
    scores, resid = pl.pallas_call(
        kernel,
        out_shape=(out, out),
        in_specs=[any_spec, any_spec, any_spec, vmem_spec, any_spec, vmem_spec],
        out_specs=(any_spec, any_spec),
        scratch_shapes=[
            V((1024, 1024), F32), V((1024, K), F32), V((1024, K), F32), V((1024, 1024), BF16),
            V((4, 512, 1024), BF16), V((4, 512, 1024), BF16), V((4, 256, 1024), BF16),
            V((1024, 512), BF16), V((1024, 256), BF16),
            V((5, 4, 256, K), F32), V((5, 2, 256, K), F32), V((5, 2, 256, K), F32), V((5, 2, 9, 32, K), F32),
            V((3, 1024, K), F32), V((3, 4, 256, K), F32), V((3, 4, 8, 32, K), F32), V((2, 1024, K), F32),
            V((4, 32, K), F32),
            V((1024, K), F32), V((1024, K), F32), V((1024, K), F32), V((1024, K), F32), V((1024, K), F32),
            V((8, 8, K), F32), V((8, 2, K), F32), V((2, 128, K), F32),
            DMA((8,)), DMA((5, 2)), DMA((5, 2)), DMA((5,)), DMA((5,)), DMA((5, 2)), DMA((3,)), DMA((3, 2, 8)),
            DMA((3,)), DMA((3, 2)), DMA((3, 2)), DMA((3,)), DMA((3, 4)), DMA((3,)), DMA((3, 4)),
            DMA((2,)), DMA((2,)), DMA((2,)), DMA((2,)), DMA((5,)),
        ],
        compiler_params=pltpu.CompilerParams(
            collective_id=0, has_side_effects=True, vmem_limit_bytes=62 * 1024 * 1024
        ),
    )(dosages, traits, start_coef, groups.reshape(8, 128), tested, owners.reshape(8, 128))
    return pl.pallas_call(
        hand_over_kernel,
        out_shape=(out, out),
        in_specs=[any_spec, any_spec],
        out_specs=(any_spec, any_spec),
        scratch_shapes=[V((4, 512, K), F32), DMA((4,)), DMA((4,))],
    )(scores, resid)


def solution(mesh):
    placed = (P("samp", "chrom"), P("samp", None), P("chrom", None), P("chrom"), P("samp", "chrom"), P("chrom"))
    return jax.shard_map(
        body, mesh=mesh, in_specs=placed, out_specs=(P("chrom", None), P("samp", None)), check_vma=False
    )
```

```python
import math

import jax
import jax.numpy as jnp
from jax import lax
from jax.experimental import pallas as pl
from jax.experimental.pallas import tpu as pltpu
from jax.sharding import PartitionSpec as P

MESH = pl.DeviceIdType.MESH
F32 = jnp.float32
BF16 = jnp.bfloat16
ITERS = 2
ROWS = 1024
K = 128
N = 8192
PENALTY = 1.5 * math.sqrt(K / N)


def remote(src, dst, send_sem, recv_sem, dev):
    return pltpu.make_async_remote_copy(
        src_ref=src, dst_ref=dst, send_sem=send_sem, recv_sem=recv_sem, device_id=dev, device_id_type=MESH
    )


def wait_bytes(ref, sem):
    pltpu.make_async_copy(ref, ref, sem).wait()


def split(value):
    high = value.astype(BF16)
    low = (value - high.astype(F32)).astype(BF16)
    return high, low


def kernel(
    dos_hbm, traits_hbm, coef_hbm, groups_ref, tested_hbm, owners_ref,
    scores_out, resid_out,
    dos, traits, coef, tested, ds, dts, tts, weights, loco_w,
    part, coresum, corebuf, crecv, rfull, gpart, grecv, gfull, score,
    acc, own0, own1, gmask, omask, tcol, tsq_recv, lsq_recv, scal,
    load_sem, core_send, core_recv, far_send, crs_send, crs_recv, cag_send, cag_recv, fwd_send, fwd_recv,
    far_recv, srs_send, srs_recv, sag_send, sag_recv, scal_send, scal_recv, small_send, small_recv, out_sem,
):
    s = lax.axis_index("samp")
    c = lax.axis_index("chrom")
    core = c % 2
    other = 1 - core
    q = c // 2
    x = q // 2
    z = q % 2
    me = s * 16 + c
    partner = (s, q * 2 + other)
    opposite = (x + 2) % 4 * 2 + (1 - z)

    def chip(dx, dz):
        return (x + dx) % 4 * 2 + (z + dz) % 2

    def samp_peer(k):
        return (s // 4 + k // 4) % 2 * 4 + (s + k) % 4

    far_first = [(2, 0), (1, 1), (3, 1), (1, 0), (3, 0), (0, 1)]
    samp_order = (6, 2, 5, 7, 3, 1, 4)

    y = s % 4
    depth = s // 4 * 2 + z
    steps = []
    for dx in range(4):
        for dy in range(4):
            for dz in range(4):
                for dc in range(2):
                    if dx + dy + dz + dc:
                        steps.append((-sum(min(d, 4 - d) for d in (dx, dy, dz)), dx, dy, dz, dc))
    everyone = []
    xs, ys, zs, cs = [[(v + d) % 4 for d in range(4)] for v in (x, y, depth)] + [[core, other]]
    s_of = [[zz // 2 * 4 + yy for yy in ys] for zz in zs]
    c_of = [[[xx * 4 + zz % 2 * 2 + cc for cc in cs] for xx in xs] for zz in zs]
    for _, dx, dy, dz, dc in sorted(steps):
        everyone.append((s_of[dz][dy], c_of[dz][dx][dc]))

    bar = pltpu.get_barrier_semaphore()
    for k in samp_order:
        pl.semaphore_signal(bar, inc=1, device_id=(samp_peer(k), c), device_id_type=MESH)
    for dx, dz in [(2, 1)] + far_first:
        pl.semaphore_signal(bar, inc=1, device_id=(s, chip(dx, dz) * 2 + core), device_id_type=MESH)
    pl.semaphore_signal(bar, inc=1, device_id=(s, opposite * 2 + other), device_id_type=MESH)
    pl.semaphore_signal(bar, inc=1, device_id=partner, device_id_type=MESH)

    order = [other * 2, other * 2 + 1, core * 2, core * 2 + 1]
    load_coef = pltpu.make_async_copy(coef_hbm, coef, load_sem.at[0])
    load_coef.start()
    load_dos = []
    for i, chunk in enumerate(order):
        rows = pl.ds(pl.multiple_of(chunk * 256, 256), 256)
        cp = pltpu.make_async_copy(dos_hbm.at[rows], dos.at[rows], load_sem.at[1 + i])
        cp.start()
        load_dos.append(cp)
    load_traits = pltpu.make_async_copy(traits_hbm, traits, load_sem.at[5])
    load_traits.start()
    load_tested = pltpu.make_async_copy(tested_hbm, tested, load_sem.at[6])
    load_tested.start()

    def set_weights(block, value, at=0):
        rows = slice(block * 128, block * 128 + 128)
        high, low = split(value)
        weights[rows, at:at + K] = high
        weights[rows, at + K:at + 2 * K] = low

    def blocks(ref):
        return [ref[b * 128:b * 128 + 128, :] for b in range(8)]

    def chunk_dot(lhs, chunk, rhs):
        out = jnp.dot(lhs[chunk], rhs, preferred_element_type=F32)
        return (out[:256, :K] + (out[:256, K:] + out[256:, K:])) + out[256:, :K]

    def rows256(chunk):
        return pl.ds(pl.multiple_of(chunk * 256, 256), 256)

    def part_dot(lhs, chunk, depth):
        out = jnp.dot(lhs[chunk, :, depth], weights[depth, 0:256], preferred_element_type=F32)
        return (out[:256, :K] + (out[:256, K:] + out[256:, K:])) + out[256:, :K]

    def rows32(t, u, half):
        return pl.ds(pl.multiple_of(half * 512 + u * 256 + t * 32, 32), 32)

    def chrom_rs(ph, compute, done, filler=None):
        cut = pl.ds(pl.multiple_of(opposite * 32, 32), 32)
        mine = pl.ds(pl.multiple_of(q * 32, 32), 32)
        for i, chunk in enumerate(order):
            u = i % 2
            part[ph, i] = compute(i, chunk)
            if i < 2:
                remote(part.at[ph, i], corebuf.at[ph, u], core_send.at[ph, u], core_recv.at[ph, u], partner).start()
                remote(part.at[ph, i, cut], crecv.at[ph, u, 8], far_send.at[ph], crs_recv.at[ph, u],
                       (s, opposite * 2 + other)).start()
            else:
                remote(part.at[ph, i, cut], crecv.at[ph, u, q], far_send.at[ph], crs_recv.at[ph, u],
                       (s, opposite * 2 + core)).start()
        for u in range(2):
            wait_bytes(corebuf.at[ph, u], core_recv.at[ph, u])
            coresum[ph, u] = part[ph, 2 + u] + corebuf[ph, u]
            for dx, dz in far_first:
                t = chip(dx, dz)
                remote(coresum.at[ph, u, pl.ds(pl.multiple_of(t * 32, 32), 32)], crecv.at[ph, u, q],
                       crs_send.at[ph], crs_recv.at[ph, u], (s, t * 2 + core)).start()
            crecv[ph, u, q] = coresum[ph, u, mine, :]
        if filler is not None:
            filler()
        for u in range(2):
            wait_bytes(crecv.at[ph, u, pl.ds(0, 8)], crs_recv.at[ph, u])
            total = crecv[ph, u, 0]
            for k in range(1, 9):
                total = total + crecv[ph, u, k]
            done(u, total)

    def chrom_ag_send(a, full, u):
        mine = rows32(q, u, core)
        remote(full.at[mine], full.at[mine], cag_send.at[a], cag_recv.at[a, u, q],
               (s, opposite * 2 + core)).start()
        remote(full.at[mine], full.at[mine], cag_send.at[a], far_recv.at[a, u],
               (s, opposite * 2 + other)).start()
        for dx, dz in far_first:
            remote(full.at[mine], full.at[mine], cag_send.at[a], cag_recv.at[a, u, q],
                   (s, chip(dx, dz) * 2 + core)).start()
        remote(full.at[mine], full.at[mine], fwd_send.at[a], fwd_recv.at[a, u], partner).start()

    def chrom_ag_wait(a, full, use):
        for u in range(2):
            for dx, dz in reversed(far_first):
                t = chip(dx, dz)
                rows = rows32(t, u, core)
                wait_bytes(full.at[rows], cag_recv.at[a, u, t])
                remote(full.at[rows], full.at[rows], fwd_send.at[a], fwd_recv.at[a, u], partner).start()
            wait_bytes(full.at[rows32(0, u, core)], cag_recv.at[a, u, opposite])
        use(core * 2)
        use(core * 2 + 1)
        for u in range(2):
            wait_bytes(full.at[rows32(0, u, core)], far_recv.at[a, u])
            wait_bytes(full.at[pl.ds(0, 224)], fwd_recv.at[a, u])
            use(other * 2 + u)

    def srows(t, u):
        return pl.ds(pl.multiple_of(u * 256 + t * 32, 32), 32)

    def samp_rs(ph, compute, done, filler=None):
        for u in range(4):
            gpart[ph, u] = compute(u)
            for k in samp_order:
                t = samp_peer(k)
                remote(gpart.at[ph, u, pl.ds(pl.multiple_of(t * 32, 32), 32)], grecv.at[ph, u, s],
                       srs_send.at[ph], srs_recv.at[ph, u], (t, c)).start()
            grecv[ph, u, s] = gpart[ph, u, pl.ds(pl.multiple_of(s * 32, 32), 32), :]
        if filler is not None:
            filler()
        for u in range(4):
            wait_bytes(grecv.at[ph, u, pl.ds(0, 7)], srs_recv.at[ph, u])
            total = grecv[ph, u, 0]
            for k in range(1, 8):
                total = total + grecv[ph, u, k]
            done(u, total)

    def samp_ag_send(ph, src, dst, u):
        for k in samp_order:
            remote(src, dst, sag_send.at[ph], sag_recv.at[ph, u], (samp_peer(k), c)).start()

    def samp_ag_wait(ph, u):
        wait_bytes(gfull.at[0, pl.ds(0, 224)], sag_recv.at[ph, u])

    def prepare_transposed():
        @pl.loop(0, 16)
        def _(b):
            i, j = b // 4, b % 4
            rows = pl.ds(pl.multiple_of(i * 256, 256), 256)
            cols = pl.ds(pl.multiple_of(j * 256, 256), 256)
            high, low = split(dos[rows, cols].T)
            dts[j, 0:256, rows] = high
            dts[j, 256:512, rows] = low

    def prepare_tested():
        load_tested.wait()

        @pl.loop(0, 16)
        def _(b):
            i, j = b // 4, b % 4
            rows = pl.ds(pl.multiple_of(i * 256, 256), 256)
            cols = pl.ds(pl.multiple_of(j * 256, 256), 256)
            tts[j, :, rows] = tested[rows, cols].astype(F32).T.astype(BF16)

    def prepare_tsq():
        for b in range(8):
            def add(i, acc):
                value = tested[pl.ds(pl.multiple_of(i * 128, 128), 128), b * 128:(b + 1) * 128].astype(F32)
                return acc + jnp.sum((value * value).reshape(16, 8, 128), axis=0)
            acc = lax.fori_loop(0, 8, add, jnp.zeros((8, 128), F32))
            tsq_recv[s, pl.ds(b, 1), :] = jnp.sum(acc, axis=0, keepdims=True)
        for k in samp_order:
            remote(tsq_recv.at[s], tsq_recv.at[s], small_send.at[0], small_recv.at[0], (samp_peer(k), c)).start()

    def prepare_masks():
        for b in range(8):
            rows = slice(b * 128, b * 128 + 128)
            g = (groups_ref[b:b + 1, :] - c * 2).astype(F32)
            gmask[rows, :] = jnp.broadcast_to(g, (128, 128)).T
            o = (owners_ref[b:b + 1, :] - c * 2).astype(F32)
            omask[rows, :] = jnp.broadcast_to(o, (128, 128)).T

    def prepare_tcol():
        wait_bytes(tsq_recv.at[pl.ds(0, 7)], small_recv.at[0])
        total = tsq_recv[0]
        for k in range(1, 8):
            total = total + tsq_recv[k]
        for b in range(8):
            tcol[b * 128:b * 128 + 128, :] = jnp.broadcast_to(total[b:b + 1, :], (128, 128)).T

    load_coef.wait()
    for b, value in enumerate(blocks(coef)):
        set_weights(b, value)

    def first_compute(i, chunk):
        load_dos[i].wait()
        high, low = split(dos[pl.ds(pl.multiple_of(chunk * 256, 256), 256), :])
        ds[chunk, 0:256, :] = high
        ds[chunk, 256:512, :] = low
        value = chunk_dot(ds, chunk, weights[:, 0:256])
        if i == 0:
            pl.semaphore_wait(bar, 16)
        return value

    def plain_compute(i, chunk):
        return chunk_dot(ds, chunk, weights[:, 0:256])

    lane = lax.broadcasted_iota(jnp.int32, (1, K), 1)

    for it in range(ITERS):
        def residual_done(u, total):
            if it == 0 and u == 0:
                load_traits.wait()
            rows = rows32(q, u, core)
            rfull[it, rows, :] = traits[rows, :] - total
            chrom_ag_send(it, rfull.at[it], u)

        chrom_rs(2 * it, first_compute if it == 0 else plain_compute, residual_done,
                 prepare_transposed if it == 0 else prepare_tsq)
        seen = []

        def use_residual(chunk):
            rows = rows256(chunk)
            high, low = split(rfull[it, rows, :])
            weights[rows, 0:K] = high
            weights[rows, K:2 * K] = low
            seen.append(rows)
            if len(seen) < 4:
                for v in range(4):
                    value = part_dot(dts, v, rows)
                    acc[v, :, 0:K] = value if len(seen) == 1 else acc[v, :, 0:K] + value

        chrom_ag_wait(it, rfull.at[it], use_residual)

        squares = []

        def gradient_done(u, total):
            grad = total * (1.0 / N)
            squares.append(jnp.sum(grad * grad, axis=0, keepdims=True))
            gfull[it, srows(s, u), :] = grad
            samp_ag_send(it, gfull.at[it, srows(s, u)], gfull.at[it, srows(s, u)], u)

        samp_rs(it, lambda v: acc[v, :, 0:K] + part_dot(dts, v, seen[3]), gradient_done,
                prepare_masks if it == 0 else prepare_tcol)
        if it == 0:
            prepare_tested()
        for u in range(4):
            samp_ag_wait(it, u)
            for b in (2 * u, 2 * u + 1):
                set_weights(b, gfull[it, b * 128:b * 128 + 128, :])
            if u < 3:
                for v in range(4):
                    value = part_dot(ds, v, slice(u * 256, u * 256 + 256))
                    acc[v, :, 0:K] = value if u == 0 else acc[v, :, 0:K] + value
        g_row = (squares[0] + squares[1]) + (squares[2] + squares[3])
        g_row = g_row + pltpu.roll(g_row, 64, 1)
        image_squares = []
        chrom_rs(2 * it + 1, lambda i, chunk: acc[chunk, :, 0:K] + part_dot(ds, chunk, slice(768, 1024)),
                 lambda u, total: image_squares.append(jnp.sum(total * total, axis=0, keepdims=True)))
        i_row = image_squares[0] + image_squares[1]
        i_row = i_row + pltpu.roll(i_row, 64, 1)
        scal[it, pl.ds(me, 1), :] = jnp.where(lane < 64, g_row, i_row)

        for far_s, far_c in everyone:
            remote(scal.at[it, pl.ds(me, 1)], scal.at[it, pl.ds(me, 1)], scal_send.at[it], scal_recv.at[it],
                   (far_s, far_c)).start()
        wait_bytes(scal.at[it, pl.ds(0, 127)], scal_recv.at[it])
        sums = jnp.sum(scal[it], axis=0, keepdims=True)
        grad_sq = jnp.sum(jnp.where(lane < 64, sums, 0.0), axis=1, keepdims=True)
        image_sq = jnp.sum(jnp.where(lane < 64, 0.0, sums), axis=1, keepdims=True)
        step = grad_sq / (image_sq * (1.0 / N) + 1e-06)
        limit = step * PENALTY
        for b in range(8):
            rows = slice(b * 128, b * 128 + 128)
            moved = coef[rows, :] + step * gfull[it, rows, :]
            length = jnp.sqrt(jnp.sum(moved * moved, axis=1, keepdims=True))
            new = moved * (jnp.maximum(length - limit, 0.0) / jnp.maximum(length, limit))
            if it + 1 < ITERS:
                coef[rows, :] = new
                set_weights(b, new)
            else:
                second = new * gmask[rows, :]
                set_weights(b, new * (1.0 - gmask[rows, :]), 0)
                set_weights(b, second, 256)

    def final_compute(i, chunk):
        rows = pl.ds(pl.multiple_of(chunk * 256, 256), 256)
        a = chunk_dot(ds, chunk, weights[:, 0:256])
        b = chunk_dot(ds, chunk, weights[:, 256:512])
        own0[rows, :] = a
        own1[rows, :] = b
        return a + b

    def last_residual_done(u, total):
        rows = rows32(q, u, core)
        rfull[2, rows, :] = traits[rows, :] - total
        chrom_ag_send(2, rfull.at[2], u)

    chrom_rs(4, final_compute, last_residual_done)
    sq = []
    seen_last = []

    def use_last(chunk):
        rows = rows256(chunk)
        res = rfull[2, rows, :]
        loco0 = res + own0[rows, :]
        loco1 = res + own1[rows, :]
        sq.append((jnp.sum(loco0 * loco0, axis=0, keepdims=True), jnp.sum(loco1 * loco1, axis=0, keepdims=True)))
        loco_w[rows, 0:K] = loco0.astype(BF16)
        loco_w[rows, K:2 * K] = loco1.astype(BF16)
        seen_last.append(rows)
        if len(seen_last) < 4:
            for v in range(4):
                value = products_of(v, rows)
                acc[v] = value if len(seen_last) == 1 else acc[v] + value

    def products_of(v, depth):
        return jnp.dot(tts[v, :, depth], loco_w[depth, :], preferred_element_type=F32)

    chrom_ag_wait(2, rfull.at[2], use_last)
    give_resid = pltpu.make_async_copy(rfull.at[2], resid_out, out_sem.at[0])
    give_resid.start()

    def products(v):
        out = acc[v] + products_of(v, seen_last[3])
        return jnp.where(omask[v * 256:v * 256 + 256, :] < 0.5, out[:, :K], out[:, K:])

    def send_squares():
        lsq_recv[s, 0:1, :] = (sq[0][0] + sq[1][0]) + (sq[2][0] + sq[3][0])
        lsq_recv[s, 1:2, :] = (sq[0][1] + sq[1][1]) + (sq[2][1] + sq[3][1])
        for k in samp_order:
            remote(lsq_recv.at[s], lsq_recv.at[s], small_send.at[1], small_recv.at[1], (samp_peer(k), c)).start()

    def score_done(u, picked):
        if u == 0:
            wait_bytes(lsq_recv.at[pl.ds(0, 7)], small_recv.at[1])
        lsum = lsq_recv[0]
        for k in range(1, 8):
            lsum = lsum + lsq_recv[k]
        rows = srows(s, u)
        lpick = jnp.where(omask[rows, :] < 0.5, lsum[0:1, :], lsum[1:2, :])
        denom = math.sqrt(N) * jnp.sqrt((tcol[rows, :] * (1.0 / N) + 1e-06) * (lpick * (1.0 / N) + 1e-06))
        score[u] = picked / denom
        samp_ag_send(2, score.at[u], scores_out.at[rows], u)
        pltpu.make_async_copy(score.at[u], scores_out.at[rows], out_sem.at[1 + u]).start()

    samp_rs(2, products, score_done, send_squares)
    for u in range(4):
        samp_ag_wait(2, u)
        wait_bytes(score.at[u], out_sem.at[1 + u])
    give_resid.wait()

    for ph in range(5):
        for u in range(2):
            wait_bytes(corebuf.at[ph, u], core_send.at[ph, u])
        wait_bytes(rfull.at[0, pl.ds(0, 128)], far_send.at[ph])
        wait_bytes(rfull.at[0, pl.ds(0, 384)], crs_send.at[ph])
    for a in range(3):
        wait_bytes(rfull.at[0, pl.ds(0, 512)], cag_send.at[a])
        wait_bytes(rfull.at[0, pl.ds(0, 448)], fwd_send.at[a])
        wait_bytes(rfull.at[0, pl.ds(0, 896)], srs_send.at[a])
        wait_bytes(rfull.at[0, pl.ds(0, 896)], sag_send.at[a])
    for it in range(ITERS):
        wait_bytes(scal.at[it, pl.ds(0, 127)], scal_send.at[it])
    wait_bytes(tsq_recv.at[pl.ds(0, 7)], small_send.at[0])
    wait_bytes(lsq_recv.at[pl.ds(0, 7)], small_send.at[1])


def hand_over_kernel(a_in, b_in, a_out, b_out, buf, in_sem, out_sem):
    pairs = [(a_in, a_out, i) for i in range(2)] + [(b_in, b_out, i) for i in range(2)]
    loads, stores = [], []
    for n, (src, _, i) in enumerate(pairs):
        loads.append(pltpu.make_async_copy(src.at[pl.ds(i * 512, 512)], buf.at[n], in_sem.at[n]))
        loads[-1].start()
    for n, (_, dst, i) in enumerate(pairs):
        loads[n].wait()
        stores.append(pltpu.make_async_copy(buf.at[n], dst.at[pl.ds(i * 512, 512)], out_sem.at[n]))
        stores[-1].start()
    for cp in stores:
        cp.wait()


def body(dosages, traits, start_coef, groups, tested, owners):
    any_spec = pl.BlockSpec(memory_space=pl.ANY)
    vmem_spec = pl.BlockSpec(memory_space=pltpu.VMEM)
    V = pltpu.VMEM
    DMA = pltpu.SemaphoreType.DMA
    out = jax.ShapeDtypeStruct((ROWS, K), F32)
    scores, resid = pl.pallas_call(
        kernel,
        out_shape=(out, out),
        in_specs=[any_spec, any_spec, any_spec, vmem_spec, any_spec, vmem_spec],
        out_specs=(any_spec, any_spec),
        scratch_shapes=[
            V((1024, 1024), F32), V((1024, K), F32), V((1024, K), F32), V((1024, 1024), BF16),
            V((4, 512, 1024), BF16), V((4, 512, 1024), BF16), V((4, 256, 1024), BF16),
            V((1024, 512), BF16), V((1024, 256), BF16),
            V((5, 4, 256, K), F32), V((5, 2, 256, K), F32), V((5, 2, 256, K), F32), V((5, 2, 9, 32, K), F32),
            V((3, 1024, K), F32), V((3, 4, 256, K), F32), V((3, 4, 8, 32, K), F32), V((2, 1024, K), F32),
            V((4, 32, K), F32), V((4, 256, 2 * K), F32),
            V((1024, K), F32), V((1024, K), F32), V((1024, K), F32), V((1024, K), F32), V((1024, K), F32),
            V((8, 8, K), F32), V((8, 2, K), F32), V((2, 128, K), F32),
            DMA((8,)), DMA((5, 2)), DMA((5, 2)), DMA((5,)), DMA((5,)), DMA((5, 2)), DMA((3,)), DMA((3, 2, 8)),
            DMA((3,)), DMA((3, 2)), DMA((3, 2)), DMA((3,)), DMA((3, 4)), DMA((3,)), DMA((3, 4)),
            DMA((2,)), DMA((2,)), DMA((2,)), DMA((2,)), DMA((5,)),
        ],
        compiler_params=pltpu.CompilerParams(
            collective_id=0, has_side_effects=True, vmem_limit_bytes=62 * 1024 * 1024
        ),
    )(dosages, traits, start_coef, groups.reshape(8, 128), tested, owners.reshape(8, 128))
    return pl.pallas_call(
        hand_over_kernel,
        out_shape=(out, out),
        in_specs=[any_spec, any_spec],
        out_specs=(any_spec, any_spec),
        scratch_shapes=[V((4, 512, K), F32), DMA((4,)), DMA((4,))],
    )(scores, resid)


def solution(mesh):
    placed = (P("samp", "chrom"), P("samp", None), P("chrom", None), P("chrom"), P("samp", "chrom"), P("chrom"))
    return jax.shard_map(
        body, mesh=mesh, in_specs=placed, out_specs=(P("chrom", None), P("samp", None)), check_vma=False
    )
```

```python
import math

import jax
import jax.numpy as jnp
from jax import lax
from jax.experimental import pallas as pl
from jax.experimental.pallas import tpu as pltpu
from jax.sharding import PartitionSpec as P

MESH = pl.DeviceIdType.MESH
F32 = jnp.float32
BF16 = jnp.bfloat16
ITERS = 2
PIECES = 2
PIECE = 64 // PIECES
PARTS = 4
PART = 128 // PARTS
ROWS = 1024
K = 128
N = 8192
PENALTY = 1.5 * math.sqrt(K / N)


def remote(src, dst, send_sem, recv_sem, dev):
    return pltpu.make_async_remote_copy(
        src_ref=src, dst_ref=dst, send_sem=send_sem, recv_sem=recv_sem, device_id=dev, device_id_type=MESH
    )


def wait_bytes(ref, sem):
    pltpu.make_async_copy(ref, ref, sem).wait()


def split(value):
    high = value.astype(BF16)
    low = (value - high.astype(F32)).astype(BF16)
    return high, low


def kernel(
    dos_hbm, traits_hbm, coef_hbm, groups_ref, tested_hbm, owners_ref,
    scores_out, resid_out,
    dos, traits, coef, tested, ds, dts, tts, weights, loco_w,
    part, coresum, corebuf, crecv, rfull, gpart, grecv, gfull, score,
    acc, own0, own1, gmask, omask, tcol, tsq_recv, lsq_recv, scal,
    load_sem, core_send, core_recv, crs_send, crs_recv, cag_send, cag_recv, fwd_send, fwd_recv,
    srs_send, srs_recv, sag_send, sag_recv, scal_send, scal_recv, small_send, small_recv, out_sem,
):
    s = lax.axis_index("samp")
    c = lax.axis_index("chrom")
    core = c % 2
    other = 1 - core
    q = c // 2
    x = q // 2
    z = q % 2
    me = s * 16 + c
    partner = (s, q * 2 + other)

    def chip(dx, dz):
        return (x + dx) % 4 * 2 + (z + dz) % 2

    def samp_peer(k):
        return (s // 4 + k // 4) % 2 * 4 + (s + k) % 4

    far_first = [(2, 1), (2, 0), (1, 1), (3, 1), (1, 0), (3, 0), (0, 1)]
    samp_order = (6, 2, 5, 7, 3, 1, 4)

    y = s % 4
    depth = s // 4 * 2 + z
    steps = []
    for dx in range(4):
        for dy in range(4):
            for dz in range(4):
                for dc in range(2):
                    if dx + dy + dz + dc:
                        steps.append((-sum(min(d, 4 - d) for d in (dx, dy, dz)), dx, dy, dz, dc))
    everyone = []
    xs, ys, zs, cs = [[(v + d) % 4 for d in range(4)] for v in (x, y, depth)] + [[core, other]]
    s_of = [[zz // 2 * 4 + yy for yy in ys] for zz in zs]
    c_of = [[[xx * 4 + zz % 2 * 2 + cc for cc in cs] for xx in xs] for zz in zs]
    for _, dx, dy, dz, dc in sorted(steps):
        everyone.append((s_of[dz][dy], c_of[dz][dx][dc]))

    bar = pltpu.get_barrier_semaphore()
    for k in samp_order:
        pl.semaphore_signal(bar, inc=1, device_id=(samp_peer(k), c), device_id_type=MESH)
    for dx, dz in far_first:
        pl.semaphore_signal(bar, inc=1, device_id=(s, chip(dx, dz) * 2 + core), device_id_type=MESH)
    pl.semaphore_signal(bar, inc=1, device_id=partner, device_id_type=MESH)

    order = [other * 2, other * 2 + 1, core * 2, core * 2 + 1]
    load_coef = pltpu.make_async_copy(coef_hbm, coef, load_sem.at[0])
    load_coef.start()
    load_dos = []
    for i, chunk in enumerate(order):
        rows = pl.ds(pl.multiple_of(chunk * 256, 256), 256)
        cp = pltpu.make_async_copy(dos_hbm.at[rows], dos.at[rows], load_sem.at[1 + i])
        cp.start()
        load_dos.append(cp)
    load_traits = pltpu.make_async_copy(traits_hbm, traits, load_sem.at[5])
    load_traits.start()
    load_tested = pltpu.make_async_copy(tested_hbm, tested, load_sem.at[6])
    load_tested.start()

    def set_weights(block, value, at=0):
        rows = slice(block * 128, block * 128 + 128)
        high, low = split(value)
        weights[rows, at:at + K] = high
        weights[rows, at + K:at + 2 * K] = low

    def blocks(ref):
        return [ref[b * 128:b * 128 + 128, :] for b in range(8)]

    def chunk_dot(lhs, chunk, rhs):
        out = jnp.dot(lhs[chunk], rhs, preferred_element_type=F32)
        return (out[:256, :K] + (out[:256, K:] + out[256:, K:])) + out[256:, :K]

    def rows256(chunk):
        return pl.ds(pl.multiple_of(chunk * 256, 256), 256)

    def part_dot(lhs, chunk, depth):
        out = jnp.dot(lhs[chunk, :, depth], weights[depth, 0:256], preferred_element_type=F32)
        return (out[:256, :K] + (out[:256, K:] + out[256:, K:])) + out[256:, :K]

    def piece(t, u, half):
        return pl.ds(pl.multiple_of(half * 512 + u * (512 // PIECES) + t * PIECE, PIECE), PIECE)

    def chrom_rs(ph, compute, done, filler=None):
        for i, chunk in enumerate(order):
            part[ph, i] = compute(i, chunk)
            if i < 2:
                remote(part.at[ph, i], corebuf.at[ph, i], core_send.at[ph, i], core_recv.at[ph, i], partner).start()
        for i in range(2):
            wait_bytes(corebuf.at[ph, i], core_recv.at[ph, i])
            coresum[ph, i * 256:i * 256 + 256, :] = part[ph, 2 + i] + corebuf[ph, i]
            for u in range(i * PIECES // 2, (i + 1) * PIECES // 2):
                for dx, dz in far_first:
                    t = chip(dx, dz)
                    remote(coresum.at[ph, piece(t, u, 0)], crecv.at[ph, u, q],
                           crs_send.at[ph], crs_recv.at[ph, u], (s, t * 2 + core)).start()
                crecv[ph, u, q] = coresum[ph, piece(q, u, 0), :]
        if filler is not None:
            filler()
        for u in range(PIECES):
            wait_bytes(crecv.at[ph, u, pl.ds(0, 7)], crs_recv.at[ph, u])
            total = crecv[ph, u, 0]
            for k in range(1, 8):
                total = total + crecv[ph, u, k]
            done(u, total)

    def chrom_ag_send(a, full, u):
        mine = piece(q, u, core)
        for dx, dz in far_first:
            remote(full.at[mine], full.at[mine], cag_send.at[a], cag_recv.at[a, u, q],
                   (s, chip(dx, dz) * 2 + core)).start()
        remote(full.at[mine], full.at[mine], fwd_send.at[a], fwd_recv.at[a, u], partner).start()

    def chrom_ag_wait(a, full, use):
        for u in range(PIECES):
            for dx, dz in reversed(far_first):
                t = chip(dx, dz)
                rows = piece(t, u, core)
                wait_bytes(full.at[rows], cag_recv.at[a, u, t])
                remote(full.at[rows], full.at[rows], fwd_send.at[a], fwd_recv.at[a, u], partner).start()
        use(core * 2)
        use(core * 2 + 1)
        for i in range(2):
            for u in range(i * PIECES // 2, (i + 1) * PIECES // 2):
                wait_bytes(full.at[pl.ds(0, 8 * PIECE)], fwd_recv.at[a, u])
            use(other * 2 + i)

    def srows(t, u):
        return pl.ds(pl.multiple_of(u * (1024 // PARTS) + t * PART, PART), PART)

    def samp_rs(ph, compute, done, filler=None):
        for v in range(4):
            gpart[ph, v * 256:v * 256 + 256, :] = compute(v)
            for u in range(v * PARTS // 4, (v + 1) * PARTS // 4):
                for k in samp_order:
                    t = samp_peer(k)
                    remote(gpart.at[ph, srows(t, u)], grecv.at[ph, u, s],
                           srs_send.at[ph], srs_recv.at[ph, u], (t, c)).start()
                grecv[ph, u, s] = gpart[ph, srows(s, u), :]
        if filler is not None:
            filler()
        for u in range(PARTS):
            wait_bytes(grecv.at[ph, u, pl.ds(0, 7)], srs_recv.at[ph, u])
            total = grecv[ph, u, 0]
            for k in range(1, 8):
                total = total + grecv[ph, u, k]
            done(u, total)

    def samp_ag_send(ph, src, dst, u):
        for k in samp_order:
            remote(src, dst, sag_send.at[ph], sag_recv.at[ph, u], (samp_peer(k), c)).start()

    def samp_ag_wait(ph, u):
        wait_bytes(gfull.at[0, pl.ds(0, 7 * PART)], sag_recv.at[ph, u])

    def prepare_transposed():
        @pl.loop(0, 16)
        def _(b):
            i, j = b // 4, b % 4
            rows = pl.ds(pl.multiple_of(i * 256, 256), 256)
            cols = pl.ds(pl.multiple_of(j * 256, 256), 256)
            high, low = split(dos[rows, cols].T)
            dts[j, 0:256, rows] = high
            dts[j, 256:512, rows] = low

    def prepare_tested():
        @pl.loop(0, 16)
        def _(b):
            i, j = b // 4, b % 4
            rows = pl.ds(pl.multiple_of(i * 256, 256), 256)
            cols = pl.ds(pl.multiple_of(j * 256, 256), 256)
            tts[j, :, rows] = tested[rows, cols].astype(F32).T.astype(BF16)

    def prepare_tsq():
        load_tested.wait()
        for b in range(8):
            def add(i, acc):
                value = tested[pl.ds(pl.multiple_of(i * 128, 128), 128), b * 128:(b + 1) * 128].astype(F32)
                return acc + jnp.sum((value * value).reshape(16, 8, 128), axis=0)
            acc = lax.fori_loop(0, 8, add, jnp.zeros((8, 128), F32))
            tsq_recv[s, pl.ds(b, 1), :] = jnp.sum(acc, axis=0, keepdims=True)
        for k in samp_order:
            remote(tsq_recv.at[s], tsq_recv.at[s], small_send.at[0], small_recv.at[0], (samp_peer(k), c)).start()

    def prepare_masks():
        for b in range(8):
            rows = slice(b * 128, b * 128 + 128)
            g = (groups_ref[b:b + 1, :] - c * 2).astype(F32)
            gmask[rows, :] = jnp.broadcast_to(g, (128, 128)).T
            o = (owners_ref[b:b + 1, :] - c * 2).astype(F32)
            omask[rows, :] = jnp.broadcast_to(o, (128, 128)).T

    def prepare_tcol():
        wait_bytes(tsq_recv.at[pl.ds(0, 7)], small_recv.at[0])
        total = tsq_recv[0]
        for k in range(1, 8):
            total = total + tsq_recv[k]
        for b in range(8):
            tcol[b * 128:b * 128 + 128, :] = jnp.broadcast_to(total[b:b + 1, :], (128, 128)).T

    load_coef.wait()
    for b, value in enumerate(blocks(coef)):
        set_weights(b, value)

    def first_compute(i, chunk):
        load_dos[i].wait()
        high, low = split(dos[pl.ds(pl.multiple_of(chunk * 256, 256), 256), :])
        ds[chunk, 0:256, :] = high
        ds[chunk, 256:512, :] = low
        value = chunk_dot(ds, chunk, weights[:, 0:256])
        if i == 0:
            pl.semaphore_wait(bar, 15)
        return value

    def plain_compute(i, chunk):
        return chunk_dot(ds, chunk, weights[:, 0:256])

    lane = lax.broadcasted_iota(jnp.int32, (1, K), 1)

    for it in range(ITERS):
        def residual_done(u, total):
            if it == 0 and u == 0:
                load_traits.wait()
            rows = piece(q, u, core)
            rfull[it, rows, :] = traits[rows, :] - total
            chrom_ag_send(it, rfull.at[it], u)

        chrom_rs(2 * it, first_compute if it == 0 else plain_compute, residual_done,
                 prepare_transposed if it == 0 else None)
        seen = []

        def use_residual(chunk):
            rows = rows256(chunk)
            high, low = split(rfull[it, rows, :])
            weights[rows, 0:K] = high
            weights[rows, K:2 * K] = low
            seen.append(rows)
            if len(seen) < 4:
                for v in range(4):
                    value = part_dot(dts, v, rows)
                    acc[v, :, 0:K] = value if len(seen) == 1 else acc[v, :, 0:K] + value

        chrom_ag_wait(it, rfull.at[it], use_residual)

        squares = []

        def gradient_done(u, total):
            grad = total * (1.0 / N)
            squares.append(jnp.sum(grad * grad, axis=0, keepdims=True))
            gfull[it, srows(s, u), :] = grad
            samp_ag_send(it, gfull.at[it, srows(s, u)], gfull.at[it, srows(s, u)], u)

        samp_rs(it, lambda v: acc[v, :, 0:K] + part_dot(dts, v, seen[3]), gradient_done)
        for u in range(4):
            for w in range(u * PARTS // 4, (u + 1) * PARTS // 4):
                samp_ag_wait(it, w)
            for b in (2 * u, 2 * u + 1):
                set_weights(b, gfull[it, b * 128:b * 128 + 128, :])
            if u < 3:
                for v in range(4):
                    value = part_dot(ds, v, slice(u * 256, u * 256 + 256))
                    acc[v, :, 0:K] = value if u == 0 else acc[v, :, 0:K] + value
        g_row = sum(squares[1:], squares[0])
        g_row = g_row + pltpu.roll(g_row, 64, 1)
        image_squares = []
        chrom_rs(2 * it + 1, lambda i, chunk: acc[chunk, :, 0:K] + part_dot(ds, chunk, slice(768, 1024)),
                 lambda u, total: image_squares.append(jnp.sum(total * total, axis=0, keepdims=True)),
                 prepare_tsq if it == 0 else None)
        i_row = sum(image_squares[1:], image_squares[0])
        i_row = i_row + pltpu.roll(i_row, 64, 1)
        scal[it, pl.ds(me, 1), :] = jnp.where(lane < 64, g_row, i_row)

        for far_s, far_c in everyone:
            remote(scal.at[it, pl.ds(me, 1)], scal.at[it, pl.ds(me, 1)], scal_send.at[it], scal_recv.at[it],
                   (far_s, far_c)).start()
        for work in ((prepare_tested,), (prepare_masks, prepare_tcol))[it]:
            work()
        wait_bytes(scal.at[it, pl.ds(0, 127)], scal_recv.at[it])
        sums = jnp.sum(scal[it], axis=0, keepdims=True)
        grad_sq = jnp.sum(jnp.where(lane < 64, sums, 0.0), axis=1, keepdims=True)
        image_sq = jnp.sum(jnp.where(lane < 64, 0.0, sums), axis=1, keepdims=True)
        step = grad_sq / (image_sq * (1.0 / N) + 1e-06)
        limit = step * PENALTY
        for b in range(8):
            rows = slice(b * 128, b * 128 + 128)
            moved = coef[rows, :] + step * gfull[it, rows, :]
            length = jnp.sqrt(jnp.sum(moved * moved, axis=1, keepdims=True))
            new = moved * (jnp.maximum(length - limit, 0.0) / jnp.maximum(length, limit))
            coef[rows, :] = new
            set_weights(b, new)

    def own_parts():
        for b in range(8):
            set_weights(b, coef[b * 128:b * 128 + 128, :] * (1.0 - gmask[b * 128:b * 128 + 128, :]), 256)
        for i, chunk in enumerate(order):
            rows = rows256(chunk)
            value = chunk_dot(ds, chunk, weights[:, 256:512])
            own0[rows, :] = value
            own1[rows, :] = part[4, i] - value

    def last_residual_done(u, total):
        rows = piece(q, u, core)
        rfull[2, rows, :] = traits[rows, :] - total
        chrom_ag_send(2, rfull.at[2], u)

    chrom_rs(4, plain_compute, last_residual_done, own_parts)
    sq = []
    seen_last = []

    def use_last(chunk):
        rows = rows256(chunk)
        res = rfull[2, rows, :]
        loco0 = res + own0[rows, :]
        loco1 = res + own1[rows, :]
        sq.append((jnp.sum(loco0 * loco0, axis=0, keepdims=True), jnp.sum(loco1 * loco1, axis=0, keepdims=True)))
        loco_w[rows, 0:K] = loco0.astype(BF16)
        loco_w[rows, K:2 * K] = loco1.astype(BF16)
        seen_last.append(rows)
        if len(seen_last) < 4:
            for v in range(4):
                value = products_of(v, rows)
                acc[v] = value if len(seen_last) == 1 else acc[v] + value

    def products_of(v, depth):
        return jnp.dot(tts[v, :, depth], loco_w[depth, :], preferred_element_type=F32)

    chrom_ag_wait(2, rfull.at[2], use_last)
    give_resid = pltpu.make_async_copy(rfull.at[2], resid_out, out_sem.at[0])
    give_resid.start()

    def products(v):
        out = acc[v] + products_of(v, seen_last[3])
        return jnp.where(omask[v * 256:v * 256 + 256, :] < 0.5, out[:, :K], out[:, K:])

    def send_squares():
        lsq_recv[s, 0:1, :] = (sq[0][0] + sq[1][0]) + (sq[2][0] + sq[3][0])
        lsq_recv[s, 1:2, :] = (sq[0][1] + sq[1][1]) + (sq[2][1] + sq[3][1])
        for k in samp_order:
            remote(lsq_recv.at[s], lsq_recv.at[s], small_send.at[1], small_recv.at[1], (samp_peer(k), c)).start()

    def score_done(u, picked):
        if u == 0:
            wait_bytes(lsq_recv.at[pl.ds(0, 7)], small_recv.at[1])
        lsum = lsq_recv[0]
        for k in range(1, 8):
            lsum = lsum + lsq_recv[k]
        rows = srows(s, u)
        lpick = jnp.where(omask[rows, :] < 0.5, lsum[0:1, :], lsum[1:2, :])
        denom = math.sqrt(N) * jnp.sqrt((tcol[rows, :] * (1.0 / N) + 1e-06) * (lpick * (1.0 / N) + 1e-06))
        score[u] = picked / denom
        samp_ag_send(2, score.at[u], scores_out.at[rows], u)
        pltpu.make_async_copy(score.at[u], scores_out.at[rows], out_sem.at[1 + u]).start()

    send_squares()
    samp_rs(2, products, score_done)
    for u in range(PARTS):
        samp_ag_wait(2, u)
        wait_bytes(score.at[u], out_sem.at[1 + u])
    give_resid.wait()

    for ph in range(5):
        for u in range(2):
            wait_bytes(corebuf.at[ph, u], core_send.at[ph, u])
        wait_bytes(rfull.at[0, pl.ds(0, 448)], crs_send.at[ph])
    for a in range(3):
        wait_bytes(rfull.at[0, pl.ds(0, 448)], cag_send.at[a])
        wait_bytes(rfull.at[0, pl.ds(0, 512)], fwd_send.at[a])
        wait_bytes(rfull.at[0, pl.ds(0, 896)], srs_send.at[a])
        wait_bytes(rfull.at[0, pl.ds(0, 896)], sag_send.at[a])
    for it in range(ITERS):
        wait_bytes(scal.at[it, pl.ds(0, 127)], scal_send.at[it])
    wait_bytes(tsq_recv.at[pl.ds(0, 7)], small_send.at[0])
    wait_bytes(lsq_recv.at[pl.ds(0, 7)], small_send.at[1])


def hand_over_kernel(a_in, b_in, a_out, b_out, buf, in_sem, out_sem):
    pairs = [(a_in, a_out, i) for i in range(2)] + [(b_in, b_out, i) for i in range(2)]
    loads, stores = [], []
    for n, (src, _, i) in enumerate(pairs):
        loads.append(pltpu.make_async_copy(src.at[pl.ds(i * 512, 512)], buf.at[n], in_sem.at[n]))
        loads[-1].start()
    for n, (_, dst, i) in enumerate(pairs):
        loads[n].wait()
        stores.append(pltpu.make_async_copy(buf.at[n], dst.at[pl.ds(i * 512, 512)], out_sem.at[n]))
        stores[-1].start()
    for cp in stores:
        cp.wait()


def body(dosages, traits, start_coef, groups, tested, owners):
    any_spec = pl.BlockSpec(memory_space=pl.ANY)
    vmem_spec = pl.BlockSpec(memory_space=pltpu.VMEM)
    V = pltpu.VMEM
    DMA = pltpu.SemaphoreType.DMA
    out = jax.ShapeDtypeStruct((ROWS, K), F32)
    scores, resid = pl.pallas_call(
        kernel,
        out_shape=(out, out),
        in_specs=[any_spec, any_spec, any_spec, vmem_spec, any_spec, vmem_spec],
        out_specs=(any_spec, any_spec),
        scratch_shapes=[
            V((1024, 1024), F32), V((1024, K), F32), V((1024, K), F32), V((1024, 1024), BF16),
            V((4, 512, 1024), BF16), V((4, 512, 1024), BF16), V((4, 256, 1024), BF16),
            V((1024, 512), BF16), V((1024, 256), BF16),
            V((5, 4, 256, K), F32), V((5, 512, K), F32), V((5, 2, 256, K), F32), V((5, PIECES, 8, PIECE, K), F32),
            V((3, 1024, K), F32), V((3, 1024, K), F32), V((3, PARTS, 8, PART, K), F32), V((2, 1024, K), F32),
            V((PARTS, PART, K), F32), V((4, 256, 2 * K), F32),
            V((1024, K), F32), V((1024, K), F32), V((1024, K), F32), V((1024, K), F32), V((1024, K), F32),
            V((8, 8, K), F32), V((8, 2, K), F32), V((2, 128, K), F32),
            DMA((8,)), DMA((5, 2)), DMA((5, 2)), DMA((5,)), DMA((5, PIECES)), DMA((3,)), DMA((3, PIECES, 8)),
            DMA((3,)), DMA((3, PIECES)), DMA((3,)), DMA((3, PARTS)), DMA((3,)), DMA((3, PARTS)),
            DMA((2,)), DMA((2,)), DMA((2,)), DMA((2,)), DMA((1 + PARTS,)),
        ],
        compiler_params=pltpu.CompilerParams(
            collective_id=0, has_side_effects=True, vmem_limit_bytes=62 * 1024 * 1024
        ),
    )(dosages, traits, start_coef, groups.reshape(8, 128), tested, owners.reshape(8, 128))
    return pl.pallas_call(
        hand_over_kernel,
        out_shape=(out, out),
        in_specs=[any_spec, any_spec],
        out_specs=(any_spec, any_spec),
        scratch_shapes=[V((4, 512, K), F32), DMA((4,)), DMA((4,))],
    )(scores, resid)


def solution(mesh):
    placed = (P("samp", "chrom"), P("samp", None), P("chrom", None), P("chrom"), P("samp", "chrom"), P("chrom"))
    return jax.shard_map(
        body, mesh=mesh, in_specs=placed, out_specs=(P("chrom", None), P("samp", None)), check_vma=False
    )
```

```python
import math

import jax
import jax.numpy as jnp
from jax import lax
from jax.experimental import pallas as pl
from jax.experimental.pallas import tpu as pltpu
from jax.sharding import PartitionSpec as P

MESH = pl.DeviceIdType.MESH
F32 = jnp.float32
BF16 = jnp.bfloat16
ITERS = 2
PIECES = 2
PIECE = 64 // PIECES
PARTS = 4
PART = 128 // PARTS
ROWS = 1024
K = 128
N = 8192
PENALTY = 1.5 * math.sqrt(K / N)


def remote(src, dst, send_sem, recv_sem, dev):
    return pltpu.make_async_remote_copy(
        src_ref=src, dst_ref=dst, send_sem=send_sem, recv_sem=recv_sem, device_id=dev, device_id_type=MESH
    )


def wait_bytes(ref, sem):
    pltpu.make_async_copy(ref, ref, sem).wait()


def split(value):
    high = value.astype(BF16)
    low = (value - high.astype(F32)).astype(BF16)
    return high, low


def kernel(
    dos_hbm, traits_hbm, coef_hbm, groups_ref, tested_hbm, owners_ref,
    scores_out, resid_out,
    dos, traits, coef, tested, ds, dts, tts, weights, loco_w,
    part, coresum, corebuf, crecv, rfull, gpart, grecv, gfull, score,
    acc, own0, own1, gmask, omask, tcol, tsq_recv, lsq_recv, scal,
    load_sem, core_send, core_recv, crs_send, crs_recv, cag_send, cag_recv, fwd_send, fwd_recv,
    srs_send, srs_recv, sag_send, sag_recv, scal_send, scal_recv, small_send, small_recv, out_sem, greet_sem,
):
    s = lax.axis_index("samp")
    c = lax.axis_index("chrom")
    core = c % 2
    other = 1 - core
    q = c // 2
    x = q // 2
    z = q % 2
    me = s * 16 + c
    partner = (s, q * 2 + other)

    def chip(dx, dz):
        return (x + dx) % 4 * 2 + (z + dz) % 2

    def samp_peer(k):
        return (s // 4 + k // 4) % 2 * 4 + (s + k) % 4

    far_first = [(2, 1), (2, 0), (1, 1), (3, 1), (1, 0), (3, 0), (0, 1)]
    samp_order = (6, 2, 5, 7, 3, 1, 4)

    y = s % 4
    depth = s // 4 * 2 + z
    steps = []
    for dx in range(4):
        for dy in range(4):
            for dz in range(4):
                for dc in range(2):
                    if dx + dy + dz + dc:
                        steps.append((-sum(min(d, 4 - d) for d in (dx, dy, dz)), dx, dy, dz, dc))
    everyone = []
    xs, ys, zs, cs = [[(v + d) % 4 for d in range(4)] for v in (x, y, depth)] + [[core, other]]
    s_of = [[zz // 2 * 4 + yy for yy in ys] for zz in zs]
    c_of = [[[xx * 4 + zz % 2 * 2 + cc for cc in cs] for xx in xs] for zz in zs]
    for _, dx, dy, dz, dc in sorted(steps):
        everyone.append((s_of[dz][dy], c_of[dz][dx][dc]))

    bar = pltpu.get_barrier_semaphore()
    near_samp = (4, 1, 3)
    for dx, dz in far_first:
        pl.semaphore_signal(bar, inc=1, device_id=(s, chip(dx, dz) * 2 + core), device_id_type=MESH)
    for k in near_samp:
        pl.semaphore_signal(bar, inc=1, device_id=(samp_peer(k), c), device_id_type=MESH)
    pl.semaphore_signal(bar, inc=1, device_id=partner, device_id_type=MESH)

    def greet(turn):
        for k in near_samp:
            pl.semaphore_signal(greet_sem.at[turn], inc=1, device_id=(samp_peer(k), c), device_id_type=MESH)

    def greeted(turn):
        pl.semaphore_wait(greet_sem.at[turn], 3)

    order = [other * 2, other * 2 + 1, core * 2, core * 2 + 1]
    load_coef = pltpu.make_async_copy(coef_hbm, coef, load_sem.at[0])
    load_coef.start()
    load_dos = []
    for i, chunk in enumerate(order):
        rows = pl.ds(pl.multiple_of(chunk * 256, 256), 256)
        load_dos.append(pltpu.make_async_copy(dos_hbm.at[rows], dos.at[rows], load_sem.at[1 + i]))
    load_dos[0].start()
    load_dos[1].start()
    load_traits = pltpu.make_async_copy(traits_hbm, traits, load_sem.at[5])
    load_tested = pltpu.make_async_copy(tested_hbm, tested, load_sem.at[6])

    def set_weights(block, value, at=0):
        rows = slice(block * 128, block * 128 + 128)
        high, low = split(value)
        weights[rows, at:at + K] = high
        weights[rows, at + K:at + 2 * K] = low

    def blocks(ref):
        return [ref[b * 128:b * 128 + 128, :] for b in range(8)]

    def chunk_dot(lhs, chunk, rhs):
        out = jnp.dot(lhs[chunk], rhs, preferred_element_type=F32)
        return (out[:256, :K] + (out[:256, K:] + out[256:, K:])) + out[256:, :K]

    def rows256(chunk):
        return pl.ds(pl.multiple_of(chunk * 256, 256), 256)

    def part_dot(lhs, chunk, depth):
        out = jnp.dot(lhs[chunk, :, depth], weights[depth, 0:256], preferred_element_type=F32)
        return (out[:256, :K] + (out[:256, K:] + out[256:, K:])) + out[256:, :K]

    def piece(t, u, half):
        return pl.ds(pl.multiple_of(half * 512 + u * (512 // PIECES) + t * PIECE, PIECE), PIECE)

    def chrom_rs(ph, compute, done, filler=None):
        def pass_on(i):
            wait_bytes(corebuf.at[ph, i], core_recv.at[ph, i])
            coresum[ph, i * 256:i * 256 + 256, :] = part[ph, 2 + i] + corebuf[ph, i]
            for u in range(i * PIECES // 2, (i + 1) * PIECES // 2):
                for dx, dz in far_first:
                    t = chip(dx, dz)
                    remote(coresum.at[ph, piece(t, u, 0)], crecv.at[ph, u, q],
                           crs_send.at[ph], crs_recv.at[ph, u], (s, t * 2 + core)).start()
                crecv[ph, u, q] = coresum[ph, piece(q, u, 0), :]

        for i, chunk in enumerate(order):
            part[ph, i] = compute(i, chunk)
            if i < 2:
                remote(part.at[ph, i], corebuf.at[ph, i], core_send.at[ph, i], core_recv.at[ph, i], partner).start()
            elif ph == 0:
                pass_on(i - 2)
        if ph > 0:
            pass_on(0)
            pass_on(1)
        if filler is not None:
            filler()
        for u in range(PIECES):
            wait_bytes(crecv.at[ph, u, pl.ds(0, 7)], crs_recv.at[ph, u])
            total = crecv[ph, u, 0]
            for k in range(1, 8):
                total = total + crecv[ph, u, k]
            done(u, total)

    def chrom_ag_send(a, full, u):
        mine = piece(q, u, core)
        for dx, dz in far_first:
            remote(full.at[mine], full.at[mine], cag_send.at[a], cag_recv.at[a, u, q],
                   (s, chip(dx, dz) * 2 + core)).start()
        remote(full.at[mine], full.at[mine], fwd_send.at[a], fwd_recv.at[a, u], partner).start()

    def chrom_ag_wait(a, full, use):
        for u in range(PIECES):
            for dx, dz in reversed(far_first):
                t = chip(dx, dz)
                rows = piece(t, u, core)
                wait_bytes(full.at[rows], cag_recv.at[a, u, t])
                remote(full.at[rows], full.at[rows], fwd_send.at[a], fwd_recv.at[a, u], partner).start()
        use(core * 2)
        use(core * 2 + 1)
        for i in range(2):
            for u in range(i * PIECES // 2, (i + 1) * PIECES // 2):
                wait_bytes(full.at[pl.ds(0, 8 * PIECE)], fwd_recv.at[a, u])
            use(other * 2 + i)

    def srows(t, u):
        return pl.ds(pl.multiple_of(u * (1024 // PARTS) + t * PART, PART), PART)

    def samp_rs(ph, compute, done, filler=None):
        for v in range(4):
            gpart[ph, v * 256:v * 256 + 256, :] = compute(v)
            for u in range(v * PARTS // 4, (v + 1) * PARTS // 4):
                for k in samp_order:
                    t = samp_peer(k)
                    remote(gpart.at[ph, srows(t, u)], grecv.at[ph, u, s],
                           srs_send.at[ph], srs_recv.at[ph, u], (t, c)).start()
                grecv[ph, u, s] = gpart[ph, srows(s, u), :]
        if filler is not None:
            filler()
        for u in range(PARTS):
            wait_bytes(grecv.at[ph, u, pl.ds(0, 7)], srs_recv.at[ph, u])
            total = grecv[ph, u, 0]
            for k in range(1, 8):
                total = total + grecv[ph, u, k]
            done(u, total)

    def samp_ag_send(ph, src, dst, u):
        for k in samp_order:
            remote(src, dst, sag_send.at[ph], sag_recv.at[ph, u], (samp_peer(k), c)).start()

    def samp_ag_wait(ph, u):
        wait_bytes(gfull.at[0, pl.ds(0, 7 * PART)], sag_recv.at[ph, u])

    def prepare_transposed():
        greet(0)
        transpose_blocks(0, 8)
        greeted(0)
        greet(1)
        transpose_blocks(8, 16)

    def transpose_blocks(first, last):
        @pl.loop(first, last)
        def _(b):
            i, j = b // 4, b % 4
            rows = pl.ds(pl.multiple_of(i * 256, 256), 256)
            cols = pl.ds(pl.multiple_of(j * 256, 256), 256)
            high, low = split(dos[rows, cols].T)
            dts[j, 0:256, rows] = high
            dts[j, 256:512, rows] = low

    def prepare_tested():
        @pl.loop(0, 16)
        def _(b):
            i, j = b // 4, b % 4
            rows = pl.ds(pl.multiple_of(i * 256, 256), 256)
            cols = pl.ds(pl.multiple_of(j * 256, 256), 256)
            tts[j, :, rows] = tested[rows, cols].astype(F32).T.astype(BF16)

    def prepare_tsq():
        load_tested.wait()
        for b in range(8):
            def add(i, acc):
                value = tested[pl.ds(pl.multiple_of(i * 128, 128), 128), b * 128:(b + 1) * 128].astype(F32)
                return acc + jnp.sum((value * value).reshape(16, 8, 128), axis=0)
            acc = lax.fori_loop(0, 8, add, jnp.zeros((8, 128), F32))
            tsq_recv[s, pl.ds(b, 1), :] = jnp.sum(acc, axis=0, keepdims=True)
        for k in samp_order:
            remote(tsq_recv.at[s], tsq_recv.at[s], small_send.at[0], small_recv.at[0], (samp_peer(k), c)).start()

    def prepare_masks():
        for b in range(8):
            rows = slice(b * 128, b * 128 + 128)
            g = (groups_ref[b:b + 1, :] - c * 2).astype(F32)
            gmask[rows, :] = jnp.broadcast_to(g, (128, 128)).T
            o = (owners_ref[b:b + 1, :] - c * 2).astype(F32)
            omask[rows, :] = jnp.broadcast_to(o, (128, 128)).T

    def prepare_tcol():
        wait_bytes(tsq_recv.at[pl.ds(0, 7)], small_recv.at[0])
        total = tsq_recv[0]
        for k in range(1, 8):
            total = total + tsq_recv[k]
        for b in range(8):
            tcol[b * 128:b * 128 + 128, :] = jnp.broadcast_to(total[b:b + 1, :], (128, 128)).T

    load_coef.wait()
    for b, value in enumerate(blocks(coef)):
        set_weights(b, value)

    def first_compute(i, chunk):
        load_dos[i].wait()
        if i < 2:
            load_dos[i + 2].start()
        if i == 2:
            load_traits.start()
        if i == 3:
            load_tested.start()
        high, low = split(dos[pl.ds(pl.multiple_of(chunk * 256, 256), 256), :])
        ds[chunk, 0:256, :] = high
        ds[chunk, 256:512, :] = low
        value = chunk_dot(ds, chunk, weights[:, 0:256])
        if i == 0:
            pl.semaphore_wait(bar, 11)
        return value

    def plain_compute(i, chunk):
        return chunk_dot(ds, chunk, weights[:, 0:256])

    lane = lax.broadcasted_iota(jnp.int32, (1, K), 1)

    for it in range(ITERS):
        def residual_done(u, total):
            if it == 0 and u == 0:
                load_traits.wait()
            rows = piece(q, u, core)
            rfull[it, rows, :] = traits[rows, :] - total
            chrom_ag_send(it, rfull.at[it], u)

        chrom_rs(2 * it, first_compute if it == 0 else plain_compute, residual_done,
                 prepare_transposed if it == 0 else None)
        seen = []

        def use_residual(chunk):
            rows = rows256(chunk)
            high, low = split(rfull[it, rows, :])
            weights[rows, 0:K] = high
            weights[rows, K:2 * K] = low
            seen.append(rows)
            if len(seen) < 4:
                for v in range(4):
                    value = part_dot(dts, v, rows)
                    acc[v, :, 0:K] = value if len(seen) == 1 else acc[v, :, 0:K] + value

        chrom_ag_wait(it, rfull.at[it], use_residual)
        if it == 0:
            greeted(1)

        squares = []

        def gradient_done(u, total):
            grad = total * (1.0 / N)
            squares.append(jnp.sum(grad * grad, axis=0, keepdims=True))
            gfull[it, srows(s, u), :] = grad
            samp_ag_send(it, gfull.at[it, srows(s, u)], gfull.at[it, srows(s, u)], u)

        samp_rs(it, lambda v: acc[v, :, 0:K] + part_dot(dts, v, seen[3]), gradient_done)
        for u in range(4):
            for w in range(u * PARTS // 4, (u + 1) * PARTS // 4):
                samp_ag_wait(it, w)
            for b in (2 * u, 2 * u + 1):
                set_weights(b, gfull[it, b * 128:b * 128 + 128, :])
            if u < 3:
                for v in range(4):
                    value = part_dot(ds, v, slice(u * 256, u * 256 + 256))
                    acc[v, :, 0:K] = value if u == 0 else acc[v, :, 0:K] + value
        g_row = sum(squares[1:], squares[0])
        g_row = g_row + pltpu.roll(g_row, 64, 1)
        image_squares = []
        chrom_rs(2 * it + 1, lambda i, chunk: acc[chunk, :, 0:K] + part_dot(ds, chunk, slice(768, 1024)),
                 lambda u, total: image_squares.append(jnp.sum(total * total, axis=0, keepdims=True)),
                 prepare_tsq if it == 0 else None)
        i_row = sum(image_squares[1:], image_squares[0])
        i_row = i_row + pltpu.roll(i_row, 64, 1)
        scal[it, pl.ds(me, 1), :] = jnp.where(lane < 64, g_row, i_row)

        for far_s, far_c in everyone:
            remote(scal.at[it, pl.ds(me, 1)], scal.at[it, pl.ds(me, 1)], scal_send.at[it], scal_recv.at[it],
                   (far_s, far_c)).start()
        for work in ((prepare_tested,), (prepare_masks, prepare_tcol))[it]:
            work()
        wait_bytes(scal.at[it, pl.ds(0, 127)], scal_recv.at[it])
        sums = jnp.sum(scal[it], axis=0, keepdims=True)
        grad_sq = jnp.sum(jnp.where(lane < 64, sums, 0.0), axis=1, keepdims=True)
        image_sq = jnp.sum(jnp.where(lane < 64, 0.0, sums), axis=1, keepdims=True)
        step = grad_sq / (image_sq * (1.0 / N) + 1e-06)
        limit = step * PENALTY
        for b in range(8):
            rows = slice(b * 128, b * 128 + 128)
            moved = coef[rows, :] + step * gfull[it, rows, :]
            length = jnp.sqrt(jnp.sum(moved * moved, axis=1, keepdims=True))
            new = moved * (jnp.maximum(length - limit, 0.0) / jnp.maximum(length, limit))
            coef[rows, :] = new
            set_weights(b, new)

    def own_parts():
        for b in range(8):
            set_weights(b, coef[b * 128:b * 128 + 128, :] * (1.0 - gmask[b * 128:b * 128 + 128, :]), 256)
        for i, chunk in enumerate(order):
            rows = rows256(chunk)
            value = chunk_dot(ds, chunk, weights[:, 256:512])
            own0[rows, :] = value
            own1[rows, :] = part[4, i] - value

    def last_residual_done(u, total):
        rows = piece(q, u, core)
        rfull[2, rows, :] = traits[rows, :] - total
        chrom_ag_send(2, rfull.at[2], u)

    chrom_rs(4, plain_compute, last_residual_done, own_parts)
    sq = []
    seen_last = []

    def use_last(chunk):
        rows = rows256(chunk)
        res = rfull[2, rows, :]
        loco0 = res + own0[rows, :]
        loco1 = res + own1[rows, :]
        sq.append((jnp.sum(loco0 * loco0, axis=0, keepdims=True), jnp.sum(loco1 * loco1, axis=0, keepdims=True)))
        loco_w[rows, 0:K] = loco0.astype(BF16)
        loco_w[rows, K:2 * K] = loco1.astype(BF16)
        seen_last.append(rows)
        if len(seen_last) < 4:
            for v in range(4):
                value = products_of(v, rows)
                acc[v] = value if len(seen_last) == 1 else acc[v] + value

    def products_of(v, depth):
        return jnp.dot(tts[v, :, depth], loco_w[depth, :], preferred_element_type=F32)

    chrom_ag_wait(2, rfull.at[2], use_last)
    give_resid = pltpu.make_async_copy(rfull.at[2], resid_out, out_sem.at[0])
    give_resid.start()

    def products(v):
        out = acc[v] + products_of(v, seen_last[3])
        return jnp.where(omask[v * 256:v * 256 + 256, :] < 0.5, out[:, :K], out[:, K:])

    def send_squares():
        lsq_recv[s, 0:1, :] = (sq[0][0] + sq[1][0]) + (sq[2][0] + sq[3][0])
        lsq_recv[s, 1:2, :] = (sq[0][1] + sq[1][1]) + (sq[2][1] + sq[3][1])
        for k in samp_order:
            remote(lsq_recv.at[s], lsq_recv.at[s], small_send.at[1], small_recv.at[1], (samp_peer(k), c)).start()

    def score_done(u, picked):
        if u == 0:
            wait_bytes(lsq_recv.at[pl.ds(0, 7)], small_recv.at[1])
        lsum = lsq_recv[0]
        for k in range(1, 8):
            lsum = lsum + lsq_recv[k]
        rows = srows(s, u)
        lpick = jnp.where(omask[rows, :] < 0.5, lsum[0:1, :], lsum[1:2, :])
        denom = math.sqrt(N) * jnp.sqrt((tcol[rows, :] * (1.0 / N) + 1e-06) * (lpick * (1.0 / N) + 1e-06))
        score[u] = picked / denom
        samp_ag_send(2, score.at[u], scores_out.at[rows], u)
        pltpu.make_async_copy(score.at[u], scores_out.at[rows], out_sem.at[1 + u]).start()

    send_squares()
    samp_rs(2, products, score_done)
    for u in range(PARTS):
        samp_ag_wait(2, u)
        wait_bytes(score.at[u], out_sem.at[1 + u])
    give_resid.wait()

    for ph in range(5):
        for u in range(2):
            wait_bytes(corebuf.at[ph, u], core_send.at[ph, u])
        wait_bytes(rfull.at[0, pl.ds(0, 448)], crs_send.at[ph])
    for a in range(3):
        wait_bytes(rfull.at[0, pl.ds(0, 448)], cag_send.at[a])
        wait_bytes(rfull.at[0, pl.ds(0, 512)], fwd_send.at[a])
        wait_bytes(rfull.at[0, pl.ds(0, 896)], srs_send.at[a])
        wait_bytes(rfull.at[0, pl.ds(0, 896)], sag_send.at[a])
    for it in range(ITERS):
        wait_bytes(scal.at[it, pl.ds(0, 127)], scal_send.at[it])
    wait_bytes(tsq_recv.at[pl.ds(0, 7)], small_send.at[0])
    wait_bytes(lsq_recv.at[pl.ds(0, 7)], small_send.at[1])


def hand_over_kernel(a_in, b_in, a_out, b_out, buf, in_sem, out_sem):
    pairs = [(a_in, a_out, i) for i in range(2)] + [(b_in, b_out, i) for i in range(2)]
    loads, stores = [], []
    for n, (src, _, i) in enumerate(pairs):
        loads.append(pltpu.make_async_copy(src.at[pl.ds(i * 512, 512)], buf.at[n], in_sem.at[n]))
        loads[-1].start()
    for n, (_, dst, i) in enumerate(pairs):
        loads[n].wait()
        stores.append(pltpu.make_async_copy(buf.at[n], dst.at[pl.ds(i * 512, 512)], out_sem.at[n]))
        stores[-1].start()
    for cp in stores:
        cp.wait()


def body(dosages, traits, start_coef, groups, tested, owners):
    any_spec = pl.BlockSpec(memory_space=pl.ANY)
    vmem_spec = pl.BlockSpec(memory_space=pltpu.VMEM)
    V = pltpu.VMEM
    DMA = pltpu.SemaphoreType.DMA
    out = jax.ShapeDtypeStruct((ROWS, K), F32)
    scores, resid = pl.pallas_call(
        kernel,
        out_shape=(out, out),
        in_specs=[any_spec, any_spec, any_spec, vmem_spec, any_spec, vmem_spec],
        out_specs=(any_spec, any_spec),
        scratch_shapes=[
            V((1024, 1024), F32), V((1024, K), F32), V((1024, K), F32), V((1024, 1024), BF16),
            V((4, 512, 1024), BF16), V((4, 512, 1024), BF16), V((4, 256, 1024), BF16),
            V((1024, 512), BF16), V((1024, 256), BF16),
            V((5, 4, 256, K), F32), V((5, 512, K), F32), V((5, 2, 256, K), F32), V((5, PIECES, 8, PIECE, K), F32),
            V((3, 1024, K), F32), V((3, 1024, K), F32), V((3, PARTS, 8, PART, K), F32), V((2, 1024, K), F32),
            V((PARTS, PART, K), F32), V((4, 256, 2 * K), F32),
            V((1024, K), F32), V((1024, K), F32), V((1024, K), F32), V((1024, K), F32), V((1024, K), F32),
            V((8, 8, K), F32), V((8, 2, K), F32), V((2, 128, K), F32),
            DMA((8,)), DMA((5, 2)), DMA((5, 2)), DMA((5,)), DMA((5, PIECES)), DMA((3,)), DMA((3, PIECES, 8)),
            DMA((3,)), DMA((3, PIECES)), DMA((3,)), DMA((3, PARTS)), DMA((3,)), DMA((3, PARTS)),
            DMA((2,)), DMA((2,)), DMA((2,)), DMA((2,)), DMA((1 + PARTS,)), pltpu.SemaphoreType.REGULAR((2,)),
        ],
        compiler_params=pltpu.CompilerParams(
            collective_id=0, has_side_effects=True, vmem_limit_bytes=62 * 1024 * 1024
        ),
    )(dosages, traits, start_coef, groups.reshape(8, 128), tested, owners.reshape(8, 128))
    return pl.pallas_call(
        hand_over_kernel,
        out_shape=(out, out),
        in_specs=[any_spec, any_spec],
        out_specs=(any_spec, any_spec),
        scratch_shapes=[V((4, 512, K), F32), DMA((4,)), DMA((4,))],
    )(scores, resid)


def solution(mesh):
    placed = (P("samp", "chrom"), P("samp", None), P("chrom", None), P("chrom"), P("samp", "chrom"), P("chrom"))
    return jax.shard_map(
        body, mesh=mesh, in_specs=placed, out_specs=(P("chrom", None), P("samp", None)), check_vma=False
    )
```

```python
import math

import jax
import jax.numpy as jnp
from jax import lax
from jax.experimental import pallas as pl
from jax.experimental.pallas import tpu as pltpu
from jax.sharding import PartitionSpec as P

MESH = pl.DeviceIdType.MESH
F32 = jnp.float32
BF16 = jnp.bfloat16
ITERS = 2
PIECES = 2
PIECE = 64 // PIECES
PARTS = 4
PART = 128 // PARTS
ROWS = 1024
K = 128
N = 8192
PENALTY = 1.5 * math.sqrt(K / N)


def remote(src, dst, send_sem, recv_sem, dev):
    return pltpu.make_async_remote_copy(
        src_ref=src, dst_ref=dst, send_sem=send_sem, recv_sem=recv_sem, device_id=dev, device_id_type=MESH
    )


def wait_bytes(ref, sem):
    pltpu.make_async_copy(ref, ref, sem).wait()


def split(value):
    high = value.astype(BF16)
    low = (value - high.astype(F32)).astype(BF16)
    return high, low


def kernel(
    dos_hbm, traits_hbm, coef_hbm, groups_hbm, tested_hbm, owners_hbm,
    scores_out, resid_out,
    groups_ref, owners_ref, dos, traits, coef, tested, ds, dts, tts, weights, loco_w,
    part, coresum, corebuf, crecv, rfull, gpart, grecv, gfull, score,
    acc, own0, own1, gmask, omask, tcol, tsq_recv, lsq_recv, scal,
    load_sem, core_send, core_recv, crs_send, crs_recv, cag_send, cag_recv, fwd_send, fwd_recv,
    srs_send, srs_recv, sag_send, sag_recv, scal_send, scal_recv, small_send, small_recv, out_sem, greet_sem,
):
    s = lax.axis_index("samp")
    c = lax.axis_index("chrom")
    core = c % 2
    other = 1 - core
    q = c // 2
    x = q // 2
    z = q % 2
    me = s * 16 + c
    partner = (s, q * 2 + other)

    def chip(dx, dz):
        return (x + dx) % 4 * 2 + (z + dz) % 2

    def samp_peer(k):
        return (s // 4 + k // 4) % 2 * 4 + (s + k) % 4

    far_first = [(2, 1), (2, 0), (1, 1), (3, 1), (1, 0), (3, 0), (0, 1)]
    samp_order = (6, 2, 5, 7, 3, 1, 4)

    y = s % 4
    depth = s // 4 * 2 + z
    steps = []
    for dx in range(4):
        for dy in range(4):
            for dz in range(4):
                for dc in range(2):
                    if dx + dy + dz + dc:
                        steps.append((-sum(min(d, 4 - d) for d in (dx, dy, dz)), dx, dy, dz, dc))
    everyone = []
    xs, ys, zs, cs = [[(v + d) % 4 for d in range(4)] for v in (x, y, depth)] + [[core, other]]
    s_of = [[zz // 2 * 4 + yy for yy in ys] for zz in zs]
    c_of = [[[xx * 4 + zz % 2 * 2 + cc for cc in cs] for xx in xs] for zz in zs]
    for _, dx, dy, dz, dc in sorted(steps):
        everyone.append((s_of[dz][dy], c_of[dz][dx][dc]))

    bar = pltpu.get_barrier_semaphore()
    near_samp = (4, 1, 3)
    for dx, dz in far_first:
        pl.semaphore_signal(bar, inc=1, device_id=(s, chip(dx, dz) * 2 + core), device_id_type=MESH)
    for k in near_samp:
        pl.semaphore_signal(bar, inc=1, device_id=(samp_peer(k), c), device_id_type=MESH)
    pl.semaphore_signal(bar, inc=1, device_id=partner, device_id_type=MESH)

    def greet(turn):
        for k in near_samp:
            pl.semaphore_signal(greet_sem.at[turn], inc=1, device_id=(samp_peer(k), c), device_id_type=MESH)

    def greeted(turn):
        pl.semaphore_wait(greet_sem.at[turn], 3)

    order = [other * 2, other * 2 + 1, core * 2, core * 2 + 1]
    load_coef = pltpu.make_async_copy(coef_hbm, coef, load_sem.at[0])
    load_coef.start()
    load_dos = []
    for i, chunk in enumerate(order):
        rows = pl.ds(pl.multiple_of(chunk * 256, 256), 256)
        load_dos.append(pltpu.make_async_copy(dos_hbm.at[rows], dos.at[rows], load_sem.at[1 + i]))
    load_dos[0].start()
    load_dos[1].start()
    load_traits = pltpu.make_async_copy(traits_hbm, traits, load_sem.at[5])
    load_tested = pltpu.make_async_copy(tested_hbm, tested, load_sem.at[6])
    load_groups = pltpu.make_async_copy(groups_hbm, groups_ref, load_sem.at[7])
    load_owners = pltpu.make_async_copy(owners_hbm, owners_ref, load_sem.at[8])

    def set_weights(block, value, at=0):
        rows = slice(block * 128, block * 128 + 128)
        high, low = split(value)
        weights[rows, at:at + K] = high
        weights[rows, at + K:at + 2 * K] = low

    def blocks(ref):
        return [ref[b * 128:b * 128 + 128, :] for b in range(8)]

    def chunk_dot(lhs, chunk, rhs):
        out = jnp.dot(lhs[chunk], rhs, preferred_element_type=F32)
        return (out[:256, :K] + (out[:256, K:] + out[256:, K:])) + out[256:, :K]

    def rows256(chunk):
        return pl.ds(pl.multiple_of(chunk * 256, 256), 256)

    def part_dot(lhs, chunk, depth):
        out = jnp.dot(lhs[chunk, :, depth], weights[depth, 0:256], preferred_element_type=F32)
        return (out[:256, :K] + (out[:256, K:] + out[256:, K:])) + out[256:, :K]

    def piece(t, u, half):
        return pl.ds(pl.multiple_of(half * 512 + u * (512 // PIECES) + t * PIECE, PIECE), PIECE)

    def chrom_rs(ph, compute, done, filler=None):
        def pass_on(i):
            wait_bytes(corebuf.at[ph, i], core_recv.at[ph, i])
            coresum[ph, i * 256:i * 256 + 256, :] = part[ph, 2 + i] + corebuf[ph, i]
            for u in range(i * PIECES // 2, (i + 1) * PIECES // 2):
                for dx, dz in far_first:
                    t = chip(dx, dz)
                    remote(coresum.at[ph, piece(t, u, 0)], crecv.at[ph, u, q],
                           crs_send.at[ph], crs_recv.at[ph, u], (s, t * 2 + core)).start()
                crecv[ph, u, q] = coresum[ph, piece(q, u, 0), :]

        for i, chunk in enumerate(order):
            part[ph, i] = compute(i, chunk)
            if i < 2:
                remote(part.at[ph, i], corebuf.at[ph, i], core_send.at[ph, i], core_recv.at[ph, i], partner).start()
            elif ph == 0:
                pass_on(i - 2)
        if ph > 0:
            pass_on(0)
            pass_on(1)
        if filler is not None:
            filler()
        for u in range(PIECES):
            wait_bytes(crecv.at[ph, u, pl.ds(0, 7)], crs_recv.at[ph, u])
            total = crecv[ph, u, 0]
            for k in range(1, 8):
                total = total + crecv[ph, u, k]
            done(u, total)

    def chrom_ag_send(a, full, u):
        mine = piece(q, u, core)
        for dx, dz in far_first:
            remote(full.at[mine], full.at[mine], cag_send.at[a], cag_recv.at[a, u, q],
                   (s, chip(dx, dz) * 2 + core)).start()
        remote(full.at[mine], full.at[mine], fwd_send.at[a], fwd_recv.at[a, u], partner).start()

    def chrom_ag_wait(a, full, use):
        for u in range(PIECES):
            for dx, dz in reversed(far_first):
                t = chip(dx, dz)
                rows = piece(t, u, core)
                wait_bytes(full.at[rows], cag_recv.at[a, u, t])
                remote(full.at[rows], full.at[rows], fwd_send.at[a], fwd_recv.at[a, u], partner).start()
        use(core * 2)
        use(core * 2 + 1)
        for i in range(2):
            for u in range(i * PIECES // 2, (i + 1) * PIECES // 2):
                wait_bytes(full.at[pl.ds(0, 8 * PIECE)], fwd_recv.at[a, u])
            use(other * 2 + i)

    def srows(t, u):
        return pl.ds(pl.multiple_of(u * (1024 // PARTS) + t * PART, PART), PART)

    def samp_rs(ph, compute, done, filler=None):
        for v in range(4):
            gpart[ph, v * 256:v * 256 + 256, :] = compute(v)
            for u in range(v * PARTS // 4, (v + 1) * PARTS // 4):
                for k in samp_order:
                    t = samp_peer(k)
                    remote(gpart.at[ph, srows(t, u)], grecv.at[ph, u, s],
                           srs_send.at[ph], srs_recv.at[ph, u], (t, c)).start()
                grecv[ph, u, s] = gpart[ph, srows(s, u), :]
        if filler is not None:
            filler()
        for u in range(PARTS):
            wait_bytes(grecv.at[ph, u, pl.ds(0, 7)], srs_recv.at[ph, u])
            total = grecv[ph, u, 0]
            for k in range(1, 8):
                total = total + grecv[ph, u, k]
            done(u, total)

    def samp_ag_send(ph, src, dst, u):
        for k in samp_order:
            remote(src, dst, sag_send.at[ph], sag_recv.at[ph, u], (samp_peer(k), c)).start()

    def samp_ag_wait(ph, u):
        wait_bytes(gfull.at[0, pl.ds(0, 7 * PART)], sag_recv.at[ph, u])

    def prepare_transposed():
        greet(0)
        transpose_blocks(0, 8)
        greeted(0)
        greet(1)
        transpose_blocks(8, 16)

    def transpose_blocks(first, last):
        @pl.loop(first, last)
        def _(b):
            i, j = b // 4, b % 4
            rows = pl.ds(pl.multiple_of(i * 256, 256), 256)
            cols = pl.ds(pl.multiple_of(j * 256, 256), 256)
            high, low = split(dos[rows, cols].T)
            dts[j, 0:256, rows] = high
            dts[j, 256:512, rows] = low

    def prepare_tested():
        @pl.loop(0, 16)
        def _(b):
            i, j = b // 4, b % 4
            rows = pl.ds(pl.multiple_of(i * 256, 256), 256)
            cols = pl.ds(pl.multiple_of(j * 256, 256), 256)
            tts[j, :, rows] = tested[rows, cols].astype(F32).T.astype(BF16)

    def prepare_tsq():
        load_tested.wait()
        for b in range(8):
            def add(i, acc):
                value = tested[pl.ds(pl.multiple_of(i * 128, 128), 128), b * 128:(b + 1) * 128].astype(F32)
                return acc + jnp.sum((value * value).reshape(16, 8, 128), axis=0)
            acc = lax.fori_loop(0, 8, add, jnp.zeros((8, 128), F32))
            tsq_recv[s, pl.ds(b, 1), :] = jnp.sum(acc, axis=0, keepdims=True)
        for k in samp_order:
            remote(tsq_recv.at[s], tsq_recv.at[s], small_send.at[0], small_recv.at[0], (samp_peer(k), c)).start()

    def prepare_masks():
        load_groups.wait()
        load_owners.wait()
        for b in range(8):
            rows = slice(b * 128, b * 128 + 128)
            g = (groups_ref[b:b + 1, :] - c * 2).astype(F32)
            gmask[rows, :] = jnp.broadcast_to(g, (128, 128)).T
            o = (owners_ref[b:b + 1, :] - c * 2).astype(F32)
            omask[rows, :] = jnp.broadcast_to(o, (128, 128)).T

    def prepare_tcol():
        wait_bytes(tsq_recv.at[pl.ds(0, 7)], small_recv.at[0])
        total = tsq_recv[0]
        for k in range(1, 8):
            total = total + tsq_recv[k]
        for b in range(8):
            tcol[b * 128:b * 128 + 128, :] = jnp.broadcast_to(total[b:b + 1, :], (128, 128)).T

    load_coef.wait()
    for b, value in enumerate(blocks(coef)):
        set_weights(b, value)

    def first_compute(i, chunk):
        load_dos[i].wait()
        if i < 2:
            load_dos[i + 2].start()
        if i == 2:
            load_traits.start()
        if i == 3:
            load_tested.start()
            load_groups.start()
            load_owners.start()
        high, low = split(dos[pl.ds(pl.multiple_of(chunk * 256, 256), 256), :])
        ds[chunk, 0:256, :] = high
        ds[chunk, 256:512, :] = low
        value = chunk_dot(ds, chunk, weights[:, 0:256])
        if i == 0:
            pl.semaphore_wait(bar, 11)
        return value

    def plain_compute(i, chunk):
        return chunk_dot(ds, chunk, weights[:, 0:256])

    lane = lax.broadcasted_iota(jnp.int32, (1, K), 1)

    for it in range(ITERS):
        def residual_done(u, total):
            if it == 0 and u == 0:
                load_traits.wait()
            rows = piece(q, u, core)
            rfull[it, rows, :] = traits[rows, :] - total
            chrom_ag_send(it, rfull.at[it], u)

        chrom_rs(2 * it, first_compute if it == 0 else plain_compute, residual_done,
                 prepare_transposed if it == 0 else None)
        seen = []

        def use_residual(chunk):
            rows = rows256(chunk)
            high, low = split(rfull[it, rows, :])
            weights[rows, 0:K] = high
            weights[rows, K:2 * K] = low
            seen.append(rows)
            if len(seen) < 4:
                for v in range(4):
                    value = part_dot(dts, v, rows)
                    acc[v, :, 0:K] = value if len(seen) == 1 else acc[v, :, 0:K] + value

        chrom_ag_wait(it, rfull.at[it], use_residual)
        if it == 0:
            greeted(1)

        squares = []

        def gradient_done(u, total):
            grad = total * (1.0 / N)
            squares.append(jnp.sum(grad * grad, axis=0, keepdims=True))
            gfull[it, srows(s, u), :] = grad
            samp_ag_send(it, gfull.at[it, srows(s, u)], gfull.at[it, srows(s, u)], u)

        samp_rs(it, lambda v: acc[v, :, 0:K] + part_dot(dts, v, seen[3]), gradient_done)
        for u in range(4):
            for w in range(u * PARTS // 4, (u + 1) * PARTS // 4):
                samp_ag_wait(it, w)
            for b in (2 * u, 2 * u + 1):
                set_weights(b, gfull[it, b * 128:b * 128 + 128, :])
            if u < 3:
                for v in range(4):
                    value = part_dot(ds, v, slice(u * 256, u * 256 + 256))
                    acc[v, :, 0:K] = value if u == 0 else acc[v, :, 0:K] + value
        g_row = sum(squares[1:], squares[0])
        g_row = g_row + pltpu.roll(g_row, 64, 1)
        image_squares = []
        chrom_rs(2 * it + 1, lambda i, chunk: acc[chunk, :, 0:K] + part_dot(ds, chunk, slice(768, 1024)),
                 lambda u, total: image_squares.append(jnp.sum(total * total, axis=0, keepdims=True)),
                 prepare_tsq if it == 0 else None)
        i_row = sum(image_squares[1:], image_squares[0])
        i_row = i_row + pltpu.roll(i_row, 64, 1)
        scal[it, pl.ds(me, 1), :] = jnp.where(lane < 64, g_row, i_row)

        for far_s, far_c in everyone:
            remote(scal.at[it, pl.ds(me, 1)], scal.at[it, pl.ds(me, 1)], scal_send.at[it], scal_recv.at[it],
                   (far_s, far_c)).start()
        for work in ((prepare_tested,), (prepare_masks, prepare_tcol))[it]:
            work()
        wait_bytes(scal.at[it, pl.ds(0, 127)], scal_recv.at[it])
        sums = jnp.sum(scal[it], axis=0, keepdims=True)
        grad_sq = jnp.sum(jnp.where(lane < 64, sums, 0.0), axis=1, keepdims=True)
        image_sq = jnp.sum(jnp.where(lane < 64, 0.0, sums), axis=1, keepdims=True)
        step = grad_sq / (image_sq * (1.0 / N) + 1e-06)
        limit = step * PENALTY
        for b in range(8):
            rows = slice(b * 128, b * 128 + 128)
            moved = coef[rows, :] + step * gfull[it, rows, :]
            length = jnp.sqrt(jnp.sum(moved * moved, axis=1, keepdims=True))
            new = moved * (jnp.maximum(length - limit, 0.0) / jnp.maximum(length, limit))
            coef[rows, :] = new
            set_weights(b, new)

    def own_parts():
        for b in range(8):
            set_weights(b, coef[b * 128:b * 128 + 128, :] * (1.0 - gmask[b * 128:b * 128 + 128, :]), 256)
        for i, chunk in enumerate(order):
            rows = rows256(chunk)
            value = chunk_dot(ds, chunk, weights[:, 256:512])
            own0[rows, :] = value
            own1[rows, :] = part[4, i] - value

    def last_residual_done(u, total):
        rows = piece(q, u, core)
        rfull[2, rows, :] = traits[rows, :] - total
        chrom_ag_send(2, rfull.at[2], u)

    chrom_rs(4, plain_compute, last_residual_done, own_parts)
    sq = []
    seen_last = []

    def use_last(chunk):
        rows = rows256(chunk)
        res = rfull[2, rows, :]
        loco0 = res + own0[rows, :]
        loco1 = res + own1[rows, :]
        sq.append((jnp.sum(loco0 * loco0, axis=0, keepdims=True), jnp.sum(loco1 * loco1, axis=0, keepdims=True)))
        loco_w[rows, 0:K] = loco0.astype(BF16)
        loco_w[rows, K:2 * K] = loco1.astype(BF16)
        seen_last.append(rows)
        if len(seen_last) < 4:
            for v in range(4):
                value = products_of(v, rows)
                acc[v] = value if len(seen_last) == 1 else acc[v] + value

    def products_of(v, depth):
        return jnp.dot(tts[v, :, depth], loco_w[depth, :], preferred_element_type=F32)

    chrom_ag_wait(2, rfull.at[2], use_last)
    give_resid = pltpu.make_async_copy(rfull.at[2], resid_out, out_sem.at[0])
    give_resid.start()

    def products(v):
        out = acc[v] + products_of(v, seen_last[3])
        return jnp.where(omask[v * 256:v * 256 + 256, :] < 0.5, out[:, :K], out[:, K:])

    def send_squares():
        lsq_recv[s, 0:1, :] = (sq[0][0] + sq[1][0]) + (sq[2][0] + sq[3][0])
        lsq_recv[s, 1:2, :] = (sq[0][1] + sq[1][1]) + (sq[2][1] + sq[3][1])
        for k in samp_order:
            remote(lsq_recv.at[s], lsq_recv.at[s], small_send.at[1], small_recv.at[1], (samp_peer(k), c)).start()

    def score_done(u, picked):
        if u == 0:
            wait_bytes(lsq_recv.at[pl.ds(0, 7)], small_recv.at[1])
        lsum = lsq_recv[0]
        for k in range(1, 8):
            lsum = lsum + lsq_recv[k]
        rows = srows(s, u)
        lpick = jnp.where(omask[rows, :] < 0.5, lsum[0:1, :], lsum[1:2, :])
        denom = math.sqrt(N) * jnp.sqrt((tcol[rows, :] * (1.0 / N) + 1e-06) * (lpick * (1.0 / N) + 1e-06))
        score[u] = picked / denom
        samp_ag_send(2, score.at[u], scores_out.at[rows], u)
        pltpu.make_async_copy(score.at[u], scores_out.at[rows], out_sem.at[1 + u]).start()

    send_squares()
    samp_rs(2, products, score_done)
    for u in range(PARTS):
        samp_ag_wait(2, u)
        wait_bytes(score.at[u], out_sem.at[1 + u])
    give_resid.wait()

    for ph in range(5):
        for u in range(2):
            wait_bytes(corebuf.at[ph, u], core_send.at[ph, u])
        wait_bytes(rfull.at[0, pl.ds(0, 448)], crs_send.at[ph])
    for a in range(3):
        wait_bytes(rfull.at[0, pl.ds(0, 448)], cag_send.at[a])
        wait_bytes(rfull.at[0, pl.ds(0, 512)], fwd_send.at[a])
        wait_bytes(rfull.at[0, pl.ds(0, 896)], srs_send.at[a])
        wait_bytes(rfull.at[0, pl.ds(0, 896)], sag_send.at[a])
    for it in range(ITERS):
        wait_bytes(scal.at[it, pl.ds(0, 127)], scal_send.at[it])
    wait_bytes(tsq_recv.at[pl.ds(0, 7)], small_send.at[0])
    wait_bytes(lsq_recv.at[pl.ds(0, 7)], small_send.at[1])


def hand_over_kernel(a_in, b_in, a_out, b_out, buf, in_sem, out_sem):
    pairs = [(a_in, a_out, i) for i in range(2)] + [(b_in, b_out, i) for i in range(2)]
    loads, stores = [], []
    for n, (src, _, i) in enumerate(pairs):
        loads.append(pltpu.make_async_copy(src.at[pl.ds(i * 512, 512)], buf.at[n], in_sem.at[n]))
        loads[-1].start()
    for n, (_, dst, i) in enumerate(pairs):
        loads[n].wait()
        stores.append(pltpu.make_async_copy(buf.at[n], dst.at[pl.ds(i * 512, 512)], out_sem.at[n]))
        stores[-1].start()
    for cp in stores:
        cp.wait()


def body(dosages, traits, start_coef, groups, tested, owners):
    any_spec = pl.BlockSpec(memory_space=pl.ANY)
    V = pltpu.VMEM
    DMA = pltpu.SemaphoreType.DMA
    out = jax.ShapeDtypeStruct((ROWS, K), F32)
    scores, resid = pl.pallas_call(
        kernel,
        out_shape=(out, out),
        in_specs=[any_spec] * 6,
        out_specs=(any_spec, any_spec),
        scratch_shapes=[
            V((8, K), jnp.int32), V((8, K), jnp.int32),
            V((1024, 1024), F32), V((1024, K), F32), V((1024, K), F32), V((1024, 1024), BF16),
            V((4, 512, 1024), BF16), V((4, 512, 1024), BF16), V((4, 256, 1024), BF16),
            V((1024, 512), BF16), V((1024, 256), BF16),
            V((5, 4, 256, K), F32), V((5, 512, K), F32), V((5, 2, 256, K), F32), V((5, PIECES, 8, PIECE, K), F32),
            V((3, 1024, K), F32), V((3, 1024, K), F32), V((3, PARTS, 8, PART, K), F32), V((2, 1024, K), F32),
            V((PARTS, PART, K), F32), V((4, 256, 2 * K), F32),
            V((1024, K), F32), V((1024, K), F32), V((1024, K), F32), V((1024, K), F32), V((1024, K), F32),
            V((8, 8, K), F32), V((8, 2, K), F32), V((2, 128, K), F32),
            DMA((9,)), DMA((5, 2)), DMA((5, 2)), DMA((5,)), DMA((5, PIECES)), DMA((3,)), DMA((3, PIECES, 8)),
            DMA((3,)), DMA((3, PIECES)), DMA((3,)), DMA((3, PARTS)), DMA((3,)), DMA((3, PARTS)),
            DMA((2,)), DMA((2,)), DMA((2,)), DMA((2,)), DMA((1 + PARTS,)), pltpu.SemaphoreType.REGULAR((2,)),
        ],
        compiler_params=pltpu.CompilerParams(
            collective_id=0, has_side_effects=True, vmem_limit_bytes=62 * 1024 * 1024
        ),
    )(dosages, traits, start_coef, groups.reshape(8, 128), tested, owners.reshape(8, 128))
    return pl.pallas_call(
        hand_over_kernel,
        out_shape=(out, out),
        in_specs=[any_spec, any_spec],
        out_specs=(any_spec, any_spec),
        scratch_shapes=[V((4, 512, K), F32), DMA((4,)), DMA((4,))],
    )(scores, resid)


def solution(mesh):
    placed = (P("samp", "chrom"), P("samp", None), P("chrom", None), P("chrom"), P("samp", "chrom"), P("chrom"))
    return jax.shard_map(
        body, mesh=mesh, in_specs=placed, out_specs=(P("chrom", None), P("samp", None)), check_vma=False
    )
```

```python
import math

import jax
import jax.numpy as jnp
from jax import lax
from jax.experimental import pallas as pl
from jax.experimental.pallas import tpu as pltpu
from jax.sharding import PartitionSpec as P

MESH = pl.DeviceIdType.MESH
F32 = jnp.float32
BF16 = jnp.bfloat16
ITERS = 2
PIECES = 2
PIECE = 64 // PIECES
PARTS = 4
PART = 128 // PARTS
ROWS = 1024
K = 128
N = 8192
PENALTY = 1.5 * math.sqrt(K / N)


def remote(src, dst, send_sem, recv_sem, dev):
    return pltpu.make_async_remote_copy(
        src_ref=src, dst_ref=dst, send_sem=send_sem, recv_sem=recv_sem, device_id=dev, device_id_type=MESH
    )


def wait_bytes(ref, sem):
    pltpu.make_async_copy(ref, ref, sem).wait()


def split(value):
    high = value.astype(BF16)
    low = (value - high.astype(F32)).astype(BF16)
    return high, low


def kernel(
    dos_hbm, traits_hbm, coef_hbm, groups_hbm, tested_hbm, owners_hbm,
    scores_out, resid_out,
    groups_ref, owners_ref, dos, traits, coef, tested, ds, dts, tts, weights, loco_w,
    part, coresum, corebuf, crecv, rfull, gpart, grecv, gfull, score,
    acc, own0, own1, gmask, omask, tcol, tsq_recv, lsq_recv, scal,
    load_sem, core_send, core_recv, crs_send, crs_recv, cag_send, cag_recv, fwd_send, fwd_recv,
    srs_send, srs_recv, sag_send, sag_recv, scal_send, scal_recv, small_send, small_recv, out_sem, greet_sem,
):
    s = lax.axis_index("samp")
    c = lax.axis_index("chrom")
    core = c % 2
    other = 1 - core
    q = c // 2
    x = q // 2
    z = q % 2
    me = s * 16 + c
    partner = (s, q * 2 + other)

    def chip(dx, dz):
        return (x + dx) % 4 * 2 + (z + dz) % 2

    def samp_peer(k):
        return (s // 4 + k // 4) % 2 * 4 + (s + k) % 4

    far_first = [(2, 1), (1, 1), (3, 1), (2, 0), (0, 1), (1, 0), (3, 0)]
    samp_order = (6, 5, 7, 2, 4, 1, 3)

    y = s % 4
    depth = s // 4 * 2 + z
    steps = []
    for dx in range(4):
        for dy in range(4):
            for dz in range(4):
                for dc in range(2):
                    if dx + dy + dz + dc:
                        steps.append((-sum(min(d, 4 - d) for d in (dx, dy, dz)), dx, dy, dz, dc))
    everyone = []
    xs, ys, zs, cs = [[(v + d) % 4 for d in range(4)] for v in (x, y, depth)] + [[core, other]]
    s_of = [[zz // 2 * 4 + yy for yy in ys] for zz in zs]
    c_of = [[[xx * 4 + zz % 2 * 2 + cc for cc in cs] for xx in xs] for zz in zs]
    for _, dx, dy, dz, dc in sorted(steps):
        everyone.append((s_of[dz][dy], c_of[dz][dx][dc]))

    bar = pltpu.get_barrier_semaphore()
    near_samp = (4, 1, 3)
    for dx, dz in far_first:
        pl.semaphore_signal(bar, inc=1, device_id=(s, chip(dx, dz) * 2 + core), device_id_type=MESH)
    for k in near_samp:
        pl.semaphore_signal(bar, inc=1, device_id=(samp_peer(k), c), device_id_type=MESH)
    pl.semaphore_signal(bar, inc=1, device_id=partner, device_id_type=MESH)

    def greet(turn):
        for k in near_samp:
            pl.semaphore_signal(greet_sem.at[turn], inc=1, device_id=(samp_peer(k), c), device_id_type=MESH)

    def greeted(turn):
        pl.semaphore_wait(greet_sem.at[turn], 3)

    order = [other * 2, other * 2 + 1, core * 2, core * 2 + 1]
    load_coef = pltpu.make_async_copy(coef_hbm, coef, load_sem.at[0])
    load_coef.start()
    load_dos = []
    for i, chunk in enumerate(order):
        rows = pl.ds(pl.multiple_of(chunk * 256, 256), 256)
        load_dos.append(pltpu.make_async_copy(dos_hbm.at[rows], dos.at[rows], load_sem.at[1 + i]))
    load_dos[0].start()
    load_dos[1].start()
    load_traits = pltpu.make_async_copy(traits_hbm, traits, load_sem.at[5])
    load_tested = pltpu.make_async_copy(tested_hbm, tested, load_sem.at[6])
    load_groups = pltpu.make_async_copy(groups_hbm, groups_ref, load_sem.at[7])
    load_owners = pltpu.make_async_copy(owners_hbm, owners_ref, load_sem.at[8])

    def set_weights(block, value, at=0):
        rows = slice(block * 128, block * 128 + 128)
        high, low = split(value)
        weights[rows, at:at + K] = high
        weights[rows, at + K:at + 2 * K] = low

    def blocks(ref):
        return [ref[b * 128:b * 128 + 128, :] for b in range(8)]

    def chunk_dot(lhs, chunk, rhs):
        out = jnp.dot(lhs[chunk], rhs, preferred_element_type=F32)
        return (out[:256, :K] + (out[:256, K:] + out[256:, K:])) + out[256:, :K]

    def rows256(chunk):
        return pl.ds(pl.multiple_of(chunk * 256, 256), 256)

    def part_dot(lhs, chunk, depth):
        out = jnp.dot(lhs[chunk, :, depth], weights[depth, 0:256], preferred_element_type=F32)
        return (out[:256, :K] + (out[:256, K:] + out[256:, K:])) + out[256:, :K]

    def piece(t, u, half):
        return pl.ds(pl.multiple_of(half * 512 + u * (512 // PIECES) + t * PIECE, PIECE), PIECE)

    def chrom_rs(ph, compute, done, filler=None):
        def pass_on(i):
            wait_bytes(corebuf.at[ph, i], core_recv.at[ph, i])
            coresum[ph, i * 256:i * 256 + 256, :] = part[ph, 2 + i] + corebuf[ph, i]
            for u in range(i * PIECES // 2, (i + 1) * PIECES // 2):
                for dx, dz in far_first:
                    t = chip(dx, dz)
                    remote(coresum.at[ph, piece(t, u, 0)], crecv.at[ph, u, q],
                           crs_send.at[ph], crs_recv.at[ph, u], (s, t * 2 + core)).start()
                crecv[ph, u, q] = coresum[ph, piece(q, u, 0), :]

        for i, chunk in enumerate(order):
            part[ph, i] = compute(i, chunk)
            if i < 2:
                remote(part.at[ph, i], corebuf.at[ph, i], core_send.at[ph, i], core_recv.at[ph, i], partner).start()
            elif ph == 0:
                pass_on(i - 2)
        if ph > 0:
            pass_on(0)
            pass_on(1)
        if filler is not None:
            filler()
        for u in range(PIECES):
            wait_bytes(crecv.at[ph, u, pl.ds(0, 7)], crs_recv.at[ph, u])
            total = crecv[ph, u, 0]
            for k in range(1, 8):
                total = total + crecv[ph, u, k]
            done(u, total)

    def chrom_ag_send(a, full, u):
        mine = piece(q, u, core)
        for dx, dz in far_first:
            remote(full.at[mine], full.at[mine], cag_send.at[a], cag_recv.at[a, u, q],
                   (s, chip(dx, dz) * 2 + core)).start()
        remote(full.at[mine], full.at[mine], fwd_send.at[a], fwd_recv.at[a, u], partner).start()

    def chrom_ag_wait(a, full, use):
        for u in range(PIECES):
            for dx, dz in reversed(far_first):
                t = chip(dx, dz)
                rows = piece(t, u, core)
                wait_bytes(full.at[rows], cag_recv.at[a, u, t])
                remote(full.at[rows], full.at[rows], fwd_send.at[a], fwd_recv.at[a, u], partner).start()
        use(core * 2)
        use(core * 2 + 1)
        for i in range(2):
            for u in range(i * PIECES // 2, (i + 1) * PIECES // 2):
                wait_bytes(full.at[pl.ds(0, 8 * PIECE)], fwd_recv.at[a, u])
            use(other * 2 + i)

    def srows(t, u):
        return pl.ds(pl.multiple_of(u * (1024 // PARTS) + t * PART, PART), PART)

    def samp_rs(ph, compute, done, filler=None):
        for v in range(4):
            gpart[ph, v * 256:v * 256 + 256, :] = compute(v)
            for u in range(v * PARTS // 4, (v + 1) * PARTS // 4):
                for k in samp_order:
                    t = samp_peer(k)
                    remote(gpart.at[ph, srows(t, u)], grecv.at[ph, u, s],
                           srs_send.at[ph], srs_recv.at[ph, u], (t, c)).start()
                grecv[ph, u, s] = gpart[ph, srows(s, u), :]
        if filler is not None:
            filler()
        for u in range(PARTS):
            wait_bytes(grecv.at[ph, u, pl.ds(0, 7)], srs_recv.at[ph, u])
            total = grecv[ph, u, 0]
            for k in range(1, 8):
                total = total + grecv[ph, u, k]
            done(u, total)

    def samp_ag_send(ph, src, dst, u):
        for k in samp_order:
            remote(src, dst, sag_send.at[ph], sag_recv.at[ph, u], (samp_peer(k), c)).start()

    def samp_ag_wait(ph, u):
        wait_bytes(gfull.at[0, pl.ds(0, 7 * PART)], sag_recv.at[ph, u])

    def prepare_transposed():
        greet(0)
        transpose_blocks(0, 8)
        greeted(0)
        greet(1)
        transpose_blocks(8, 16)

    def transpose_blocks(first, last):
        @pl.loop(first, last)
        def _(b):
            i, j = b // 4, b % 4
            rows = pl.ds(pl.multiple_of(i * 256, 256), 256)
            cols = pl.ds(pl.multiple_of(j * 256, 256), 256)
            high, low = split(dos[rows, cols].T)
            dts[j, 0:256, rows] = high
            dts[j, 256:512, rows] = low

    def prepare_tested():
        @pl.loop(0, 16)
        def _(b):
            i, j = b // 4, b % 4
            rows = pl.ds(pl.multiple_of(i * 256, 256), 256)
            cols = pl.ds(pl.multiple_of(j * 256, 256), 256)
            tts[j, :, rows] = tested[rows, cols].astype(F32).T.astype(BF16)

    def prepare_tsq():
        load_tested.wait()
        for b in range(8):
            def add(i, acc):
                value = tested[pl.ds(pl.multiple_of(i * 128, 128), 128), b * 128:(b + 1) * 128].astype(F32)
                return acc + jnp.sum((value * value).reshape(16, 8, 128), axis=0)
            acc = lax.fori_loop(0, 8, add, jnp.zeros((8, 128), F32))
            tsq_recv[s, pl.ds(b, 1), :] = jnp.sum(acc, axis=0, keepdims=True)
        for k in samp_order:
            remote(tsq_recv.at[s], tsq_recv.at[s], small_send.at[0], small_recv.at[0], (samp_peer(k), c)).start()

    def prepare_masks():
        load_groups.wait()
        load_owners.wait()
        for b in range(8):
            rows = slice(b * 128, b * 128 + 128)
            g = (groups_ref[b:b + 1, :] - c * 2).astype(F32)
            gmask[rows, :] = jnp.broadcast_to(g, (128, 128)).T
            o = (owners_ref[b:b + 1, :] - c * 2).astype(F32)
            omask[rows, :] = jnp.broadcast_to(o, (128, 128)).T

    def prepare_tcol():
        wait_bytes(tsq_recv.at[pl.ds(0, 7)], small_recv.at[0])
        total = tsq_recv[0]
        for k in range(1, 8):
            total = total + tsq_recv[k]
        for b in range(8):
            tcol[b * 128:b * 128 + 128, :] = jnp.broadcast_to(total[b:b + 1, :], (128, 128)).T

    load_coef.wait()
    for b, value in enumerate(blocks(coef)):
        set_weights(b, value)

    def first_compute(i, chunk):
        load_dos[i].wait()
        if i < 2:
            load_dos[i + 2].start()
        if i == 2:
            load_traits.start()
        if i == 3:
            load_tested.start()
            load_groups.start()
            load_owners.start()
        high, low = split(dos[pl.ds(pl.multiple_of(chunk * 256, 256), 256), :])
        ds[chunk, 0:256, :] = high
        ds[chunk, 256:512, :] = low
        value = chunk_dot(ds, chunk, weights[:, 0:256])
        if i == 0:
            pl.semaphore_wait(bar, 11)
        return value

    def plain_compute(i, chunk):
        return chunk_dot(ds, chunk, weights[:, 0:256])

    lane = lax.broadcasted_iota(jnp.int32, (1, K), 1)

    for it in range(ITERS):
        def residual_done(u, total):
            if it == 0 and u == 0:
                load_traits.wait()
            rows = piece(q, u, core)
            rfull[it, rows, :] = traits[rows, :] - total
            chrom_ag_send(it, rfull.at[it], u)

        chrom_rs(2 * it, first_compute if it == 0 else plain_compute, residual_done,
                 prepare_transposed if it == 0 else None)
        seen = []

        def use_residual(chunk):
            rows = rows256(chunk)
            high, low = split(rfull[it, rows, :])
            weights[rows, 0:K] = high
            weights[rows, K:2 * K] = low
            seen.append(rows)
            if len(seen) < 4:
                for v in range(4):
                    value = part_dot(dts, v, rows)
                    acc[v, :, 0:K] = value if len(seen) == 1 else acc[v, :, 0:K] + value

        chrom_ag_wait(it, rfull.at[it], use_residual)
        if it == 0:
            greeted(1)

        squares = []

        def gradient_done(u, total):
            grad = total * (1.0 / N)
            squares.append(jnp.sum(grad * grad, axis=0, keepdims=True))
            gfull[it, srows(s, u), :] = grad
            samp_ag_send(it, gfull.at[it, srows(s, u)], gfull.at[it, srows(s, u)], u)

        samp_rs(it, lambda v: acc[v, :, 0:K] + part_dot(dts, v, seen[3]), gradient_done)
        for u in range(4):
            for w in range(u * PARTS // 4, (u + 1) * PARTS // 4):
                samp_ag_wait(it, w)
            for b in (2 * u, 2 * u + 1):
                set_weights(b, gfull[it, b * 128:b * 128 + 128, :])
            if u < 3:
                for v in range(4):
                    value = part_dot(ds, v, slice(u * 256, u * 256 + 256))
                    acc[v, :, 0:K] = value if u == 0 else acc[v, :, 0:K] + value
        g_row = sum(squares[1:], squares[0])
        g_row = g_row + pltpu.roll(g_row, 64, 1)
        image_squares = []
        chrom_rs(2 * it + 1, lambda i, chunk: acc[chunk, :, 0:K] + part_dot(ds, chunk, slice(768, 1024)),
                 lambda u, total: image_squares.append(jnp.sum(total * total, axis=0, keepdims=True)),
                 prepare_tsq if it == 0 else None)
        i_row = sum(image_squares[1:], image_squares[0])
        i_row = i_row + pltpu.roll(i_row, 64, 1)
        scal[it, pl.ds(me, 1), :] = jnp.where(lane < 64, g_row, i_row)

        for far_s, far_c in everyone:
            remote(scal.at[it, pl.ds(me, 1)], scal.at[it, pl.ds(me, 1)], scal_send.at[it], scal_recv.at[it],
                   (far_s, far_c)).start()
        for work in ((prepare_tested,), (prepare_masks, prepare_tcol))[it]:
            work()
        wait_bytes(scal.at[it, pl.ds(0, 127)], scal_recv.at[it])
        sums = jnp.sum(scal[it], axis=0, keepdims=True)
        grad_sq = jnp.sum(jnp.where(lane < 64, sums, 0.0), axis=1, keepdims=True)
        image_sq = jnp.sum(jnp.where(lane < 64, 0.0, sums), axis=1, keepdims=True)
        step = grad_sq / (image_sq * (1.0 / N) + 1e-06)
        limit = step * PENALTY
        for b in range(8):
            rows = slice(b * 128, b * 128 + 128)
            moved = coef[rows, :] + step * gfull[it, rows, :]
            length = jnp.sqrt(jnp.sum(moved * moved, axis=1, keepdims=True))
            new = moved * (jnp.maximum(length - limit, 0.0) / jnp.maximum(length, limit))
            coef[rows, :] = new
            set_weights(b, new)

    def own_parts():
        for b in range(8):
            set_weights(b, coef[b * 128:b * 128 + 128, :] * (1.0 - gmask[b * 128:b * 128 + 128, :]), 256)
        for i, chunk in enumerate(order):
            rows = rows256(chunk)
            value = chunk_dot(ds, chunk, weights[:, 256:512])
            own0[rows, :] = value
            own1[rows, :] = part[4, i] - value

    def last_residual_done(u, total):
        rows = piece(q, u, core)
        rfull[2, rows, :] = traits[rows, :] - total
        chrom_ag_send(2, rfull.at[2], u)

    chrom_rs(4, plain_compute, last_residual_done, own_parts)
    sq = []
    seen_last = []

    def use_last(chunk):
        rows = rows256(chunk)
        res = rfull[2, rows, :]
        loco0 = res + own0[rows, :]
        loco1 = res + own1[rows, :]
        sq.append((jnp.sum(loco0 * loco0, axis=0, keepdims=True), jnp.sum(loco1 * loco1, axis=0, keepdims=True)))
        loco_w[rows, 0:K] = loco0.astype(BF16)
        loco_w[rows, K:2 * K] = loco1.astype(BF16)
        seen_last.append(rows)
        if len(seen_last) < 4:
            for v in range(4):
                value = products_of(v, rows)
                acc[v] = value if len(seen_last) == 1 else acc[v] + value

    def products_of(v, depth):
        return jnp.dot(tts[v, :, depth], loco_w[depth, :], preferred_element_type=F32)

    chrom_ag_wait(2, rfull.at[2], use_last)
    give_resid = pltpu.make_async_copy(rfull.at[2], resid_out, out_sem.at[0])
    give_resid.start()

    def products(v):
        out = acc[v] + products_of(v, seen_last[3])
        return jnp.where(omask[v * 256:v * 256 + 256, :] < 0.5, out[:, :K], out[:, K:])

    def send_squares():
        lsq_recv[s, 0:1, :] = (sq[0][0] + sq[1][0]) + (sq[2][0] + sq[3][0])
        lsq_recv[s, 1:2, :] = (sq[0][1] + sq[1][1]) + (sq[2][1] + sq[3][1])
        for k in samp_order:
            remote(lsq_recv.at[s], lsq_recv.at[s], small_send.at[1], small_recv.at[1], (samp_peer(k), c)).start()

    def score_done(u, picked):
        if u == 0:
            wait_bytes(lsq_recv.at[pl.ds(0, 7)], small_recv.at[1])
        lsum = lsq_recv[0]
        for k in range(1, 8):
            lsum = lsum + lsq_recv[k]
        rows = srows(s, u)
        lpick = jnp.where(omask[rows, :] < 0.5, lsum[0:1, :], lsum[1:2, :])
        denom = math.sqrt(N) * jnp.sqrt((tcol[rows, :] * (1.0 / N) + 1e-06) * (lpick * (1.0 / N) + 1e-06))
        score[u] = picked / denom
        samp_ag_send(2, score.at[u], scores_out.at[rows], u)
        pltpu.make_async_copy(score.at[u], scores_out.at[rows], out_sem.at[1 + u]).start()

    send_squares()
    samp_rs(2, products, score_done)
    for u in range(PARTS):
        samp_ag_wait(2, u)
        wait_bytes(score.at[u], out_sem.at[1 + u])
    give_resid.wait()

    for ph in range(5):
        for u in range(2):
            wait_bytes(corebuf.at[ph, u], core_send.at[ph, u])
        wait_bytes(rfull.at[0, pl.ds(0, 448)], crs_send.at[ph])
    for a in range(3):
        wait_bytes(rfull.at[0, pl.ds(0, 448)], cag_send.at[a])
        wait_bytes(rfull.at[0, pl.ds(0, 512)], fwd_send.at[a])
        wait_bytes(rfull.at[0, pl.ds(0, 896)], srs_send.at[a])
        wait_bytes(rfull.at[0, pl.ds(0, 896)], sag_send.at[a])
    for it in range(ITERS):
        wait_bytes(scal.at[it, pl.ds(0, 127)], scal_send.at[it])
    wait_bytes(tsq_recv.at[pl.ds(0, 7)], small_send.at[0])
    wait_bytes(lsq_recv.at[pl.ds(0, 7)], small_send.at[1])


def hand_over_kernel(a_in, b_in, a_out, b_out, buf, in_sem, out_sem):
    pairs = [(a_in, a_out, i) for i in range(2)] + [(b_in, b_out, i) for i in range(2)]
    loads, stores = [], []
    for n, (src, _, i) in enumerate(pairs):
        loads.append(pltpu.make_async_copy(src.at[pl.ds(i * 512, 512)], buf.at[n], in_sem.at[n]))
        loads[-1].start()
    for n, (_, dst, i) in enumerate(pairs):
        loads[n].wait()
        stores.append(pltpu.make_async_copy(buf.at[n], dst.at[pl.ds(i * 512, 512)], out_sem.at[n]))
        stores[-1].start()
    for cp in stores:
        cp.wait()


def body(dosages, traits, start_coef, groups, tested, owners):
    any_spec = pl.BlockSpec(memory_space=pl.ANY)
    V = pltpu.VMEM
    DMA = pltpu.SemaphoreType.DMA
    out = jax.ShapeDtypeStruct((ROWS, K), F32)
    scores, resid = pl.pallas_call(
        kernel,
        out_shape=(out, out),
        in_specs=[any_spec] * 6,
        out_specs=(any_spec, any_spec),
        scratch_shapes=[
            V((8, K), jnp.int32), V((8, K), jnp.int32),
            V((1024, 1024), F32), V((1024, K), F32), V((1024, K), F32), V((1024, 1024), BF16),
            V((4, 512, 1024), BF16), V((4, 512, 1024), BF16), V((4, 256, 1024), BF16),
            V((1024, 512), BF16), V((1024, 256), BF16),
            V((5, 4, 256, K), F32), V((5, 512, K), F32), V((5, 2, 256, K), F32), V((5, PIECES, 8, PIECE, K), F32),
            V((3, 1024, K), F32), V((3, 1024, K), F32), V((3, PARTS, 8, PART, K), F32), V((2, 1024, K), F32),
            V((PARTS, PART, K), F32), V((4, 256, 2 * K), F32),
            V((1024, K), F32), V((1024, K), F32), V((1024, K), F32), V((1024, K), F32), V((1024, K), F32),
            V((8, 8, K), F32), V((8, 2, K), F32), V((2, 128, K), F32),
            DMA((9,)), DMA((5, 2)), DMA((5, 2)), DMA((5,)), DMA((5, PIECES)), DMA((3,)), DMA((3, PIECES, 8)),
            DMA((3,)), DMA((3, PIECES)), DMA((3,)), DMA((3, PARTS)), DMA((3,)), DMA((3, PARTS)),
            DMA((2,)), DMA((2,)), DMA((2,)), DMA((2,)), DMA((1 + PARTS,)), pltpu.SemaphoreType.REGULAR((2,)),
        ],
        compiler_params=pltpu.CompilerParams(
            collective_id=0, has_side_effects=True, vmem_limit_bytes=62 * 1024 * 1024
        ),
    )(dosages, traits, start_coef, groups.reshape(8, 128), tested, owners.reshape(8, 128))
    return pl.pallas_call(
        hand_over_kernel,
        out_shape=(out, out),
        in_specs=[any_spec, any_spec],
        out_specs=(any_spec, any_spec),
        scratch_shapes=[V((4, 512, K), F32), DMA((4,)), DMA((4,))],
    )(scores, resid)


def solution(mesh):
    placed = (P("samp", "chrom"), P("samp", None), P("chrom", None), P("chrom"), P("samp", "chrom"), P("chrom"))
    return jax.shard_map(
        body, mesh=mesh, in_specs=placed, out_specs=(P("chrom", None), P("samp", None)), check_vma=False
    )
```

```python
import math

import jax
import jax.numpy as jnp
from jax import lax
from jax.experimental import pallas as pl
from jax.experimental.pallas import tpu as pltpu
from jax.sharding import PartitionSpec as P

MESH = pl.DeviceIdType.MESH
F32 = jnp.float32
BF16 = jnp.bfloat16
ITERS = 2
PIECES = 2
PIECE = 64 // PIECES
PARTS = 4
PART = 128 // PARTS
ROWS = 1024
K = 128
N = 8192
PENALTY = 1.5 * math.sqrt(K / N)


def remote(src, dst, send_sem, recv_sem, dev):
    return pltpu.make_async_remote_copy(
        src_ref=src, dst_ref=dst, send_sem=send_sem, recv_sem=recv_sem, device_id=dev, device_id_type=MESH
    )


def wait_bytes(ref, sem):
    pltpu.make_async_copy(ref, ref, sem).wait()


def split(value):
    high = value.astype(BF16)
    low = (value - high.astype(F32)).astype(BF16)
    return high, low


def kernel(
    dos_hbm, traits_hbm, coef_hbm, groups_hbm, tested_hbm, owners_hbm,
    scores_out, resid_out,
    groups_ref, owners_ref, dos, traits, coef, tested, ds, dts, tts, weights, loco_w,
    part, coresum, corebuf, crecv, rfull, gpart, grecv, gfull, score,
    acc, own0, own1, gmask, omask, tcol, tsq_recv, lsq_recv, scal,
    load_sem, core_send, core_recv, crs_send, crs_recv, cag_send, cag_recv, fwd_send, fwd_recv,
    srs_send, srs_recv, sag_send, sag_recv, scal_send, scal_recv, small_send, small_recv, out_sem, greet_sem,
):
    s = lax.axis_index("samp")
    c = lax.axis_index("chrom")
    core = c % 2
    other = 1 - core
    q = c // 2
    x = q // 2
    z = q % 2
    me = s * 16 + c
    partner = (s, q * 2 + other)

    def chip(dx, dz):
        return (x + dx) % 4 * 2 + (z + dz) % 2

    def samp_peer(k):
        return (s // 4 + k // 4) % 2 * 4 + (s + k) % 4

    far_first = [(2, 1), (1, 1), (3, 1), (0, 1), (2, 0), (1, 0), (3, 0)]
    samp_order = (6, 5, 7, 4, 2, 1, 3)

    y = s % 4
    depth = s // 4 * 2 + z
    steps = []
    for dx in range(4):
        for dy in range(4):
            for dz in range(4):
                for dc in range(2):
                    if dx + dy + dz + dc:
                        steps.append((-sum(min(d, 4 - d) for d in (dx, dy, dz)), dx, dy, dz, dc))
    everyone = []
    xs, ys, zs, cs = [[(v + d) % 4 for d in range(4)] for v in (x, y, depth)] + [[core, other]]
    s_of = [[zz // 2 * 4 + yy for yy in ys] for zz in zs]
    c_of = [[[xx * 4 + zz % 2 * 2 + cc for cc in cs] for xx in xs] for zz in zs]
    for _, dx, dy, dz, dc in sorted(steps):
        everyone.append((s_of[dz][dy], c_of[dz][dx][dc]))

    bar = pltpu.get_barrier_semaphore()
    near_samp = (4, 1, 3)
    for dx, dz in far_first:
        pl.semaphore_signal(bar, inc=1, device_id=(s, chip(dx, dz) * 2 + core), device_id_type=MESH)
    for k in near_samp:
        pl.semaphore_signal(bar, inc=1, device_id=(samp_peer(k), c), device_id_type=MESH)
    pl.semaphore_signal(bar, inc=1, device_id=partner, device_id_type=MESH)

    def greet(turn):
        for k in near_samp:
            pl.semaphore_signal(greet_sem.at[turn], inc=1, device_id=(samp_peer(k), c), device_id_type=MESH)

    def greeted(turn):
        pl.semaphore_wait(greet_sem.at[turn], 3)

    order = [other * 2, other * 2 + 1, core * 2, core * 2 + 1]
    load_coef = pltpu.make_async_copy(coef_hbm, coef, load_sem.at[0])
    load_coef.start()
    load_dos = []
    for i, chunk in enumerate(order):
        rows = pl.ds(pl.multiple_of(chunk * 256, 256), 256)
        load_dos.append(pltpu.make_async_copy(dos_hbm.at[rows], dos.at[rows], load_sem.at[1 + i]))
    load_dos[0].start()
    load_dos[1].start()
    load_traits = pltpu.make_async_copy(traits_hbm, traits, load_sem.at[5])
    load_tested = pltpu.make_async_copy(tested_hbm, tested, load_sem.at[6])
    load_groups = pltpu.make_async_copy(groups_hbm, groups_ref, load_sem.at[7])
    load_owners = pltpu.make_async_copy(owners_hbm, owners_ref, load_sem.at[8])

    def set_weights(block, value, at=0):
        rows = slice(block * 128, block * 128 + 128)
        high, low = split(value)
        weights[rows, at:at + K] = high
        weights[rows, at + K:at + 2 * K] = low

    def blocks(ref):
        return [ref[b * 128:b * 128 + 128, :] for b in range(8)]

    def chunk_dot(lhs, chunk, rhs):
        out = jnp.dot(lhs[chunk], rhs, preferred_element_type=F32)
        return (out[:256, :K] + (out[:256, K:] + out[256:, K:])) + out[256:, :K]

    def rows256(chunk):
        return pl.ds(pl.multiple_of(chunk * 256, 256), 256)

    def part_dot(lhs, chunk, depth):
        out = jnp.dot(lhs[chunk, :, depth], weights[depth, 0:256], preferred_element_type=F32)
        return (out[:256, :K] + (out[:256, K:] + out[256:, K:])) + out[256:, :K]

    def piece(t, u, half):
        return pl.ds(pl.multiple_of(half * 512 + u * (512 // PIECES) + t * PIECE, PIECE), PIECE)

    def chrom_rs(ph, compute, done, filler=None):
        def pass_on(i):
            wait_bytes(corebuf.at[ph, i], core_recv.at[ph, i])
            coresum[ph, i * 256:i * 256 + 256, :] = part[ph, 2 + i] + corebuf[ph, i]
            for u in range(i * PIECES // 2, (i + 1) * PIECES // 2):
                for dx, dz in far_first:
                    t = chip(dx, dz)
                    remote(coresum.at[ph, piece(t, u, 0)], crecv.at[ph, u, q],
                           crs_send.at[ph], crs_recv.at[ph, u], (s, t * 2 + core)).start()
                crecv[ph, u, q] = coresum[ph, piece(q, u, 0), :]

        for i, chunk in enumerate(order):
            part[ph, i] = compute(i, chunk)
            if i < 2:
                remote(part.at[ph, i], corebuf.at[ph, i], core_send.at[ph, i], core_recv.at[ph, i], partner).start()
            elif ph == 0:
                pass_on(i - 2)
        if ph > 0:
            pass_on(0)
            pass_on(1)
        if filler is not None:
            filler()
        for u in range(PIECES):
            wait_bytes(crecv.at[ph, u, pl.ds(0, 7)], crs_recv.at[ph, u])
            total = crecv[ph, u, 0]
            for k in range(1, 8):
                total = total + crecv[ph, u, k]
            done(u, total)

    def chrom_ag_send(a, full, u):
        mine = piece(q, u, core)
        for dx, dz in far_first:
            remote(full.at[mine], full.at[mine], cag_send.at[a], cag_recv.at[a, u, q],
                   (s, chip(dx, dz) * 2 + core)).start()
        remote(full.at[mine], full.at[mine], fwd_send.at[a], fwd_recv.at[a, u], partner).start()

    def chrom_ag_wait(a, full, use):
        for u in range(PIECES):
            for dx, dz in reversed(far_first):
                t = chip(dx, dz)
                rows = piece(t, u, core)
                wait_bytes(full.at[rows], cag_recv.at[a, u, t])
                remote(full.at[rows], full.at[rows], fwd_send.at[a], fwd_recv.at[a, u], partner).start()
        use(core * 2)
        use(core * 2 + 1)
        for i in range(2):
            for u in range(i * PIECES // 2, (i + 1) * PIECES // 2):
                wait_bytes(full.at[pl.ds(0, 8 * PIECE)], fwd_recv.at[a, u])
            use(other * 2 + i)

    def srows(t, u):
        return pl.ds(pl.multiple_of(u * (1024 // PARTS) + t * PART, PART), PART)

    def samp_rs(ph, compute, done, filler=None):
        for v in range(4):
            gpart[ph, v * 256:v * 256 + 256, :] = compute(v)
            for u in range(v * PARTS // 4, (v + 1) * PARTS // 4):
                for k in samp_order:
                    t = samp_peer(k)
                    remote(gpart.at[ph, srows(t, u)], grecv.at[ph, u, s],
                           srs_send.at[ph], srs_recv.at[ph, u], (t, c)).start()
                grecv[ph, u, s] = gpart[ph, srows(s, u), :]
        if filler is not None:
            filler()
        for u in range(PARTS):
            wait_bytes(grecv.at[ph, u, pl.ds(0, 7)], srs_recv.at[ph, u])
            total = grecv[ph, u, 0]
            for k in range(1, 8):
                total = total + grecv[ph, u, k]
            done(u, total)

    def samp_ag_send(ph, src, dst, u):
        for k in samp_order:
            remote(src, dst, sag_send.at[ph], sag_recv.at[ph, u], (samp_peer(k), c)).start()

    def samp_ag_wait(ph, u):
        wait_bytes(gfull.at[0, pl.ds(0, 7 * PART)], sag_recv.at[ph, u])

    def prepare_transposed():
        greet(0)
        transpose_blocks(0, 8)
        greeted(0)
        greet(1)
        transpose_blocks(8, 16)

    def transpose_blocks(first, last):
        @pl.loop(first, last)
        def _(b):
            i, j = b // 4, b % 4
            rows = pl.ds(pl.multiple_of(i * 256, 256), 256)
            cols = pl.ds(pl.multiple_of(j * 256, 256), 256)
            high, low = split(dos[rows, cols].T)
            dts[j, 0:256, rows] = high
            dts[j, 256:512, rows] = low

    def prepare_tested():
        @pl.loop(0, 16)
        def _(b):
            i, j = b // 4, b % 4
            rows = pl.ds(pl.multiple_of(i * 256, 256), 256)
            cols = pl.ds(pl.multiple_of(j * 256, 256), 256)
            tts[j, :, rows] = tested[rows, cols].astype(F32).T.astype(BF16)

    def prepare_tsq():
        load_tested.wait()
        for b in range(8):
            def add(i, acc):
                value = tested[pl.ds(pl.multiple_of(i * 128, 128), 128), b * 128:(b + 1) * 128].astype(F32)
                return acc + jnp.sum((value * value).reshape(16, 8, 128), axis=0)
            acc = lax.fori_loop(0, 8, add, jnp.zeros((8, 128), F32))
            tsq_recv[s, pl.ds(b, 1), :] = jnp.sum(acc, axis=0, keepdims=True)
        for k in samp_order:
            remote(tsq_recv.at[s], tsq_recv.at[s], small_send.at[0], small_recv.at[0], (samp_peer(k), c)).start()

    def prepare_masks():
        load_groups.wait()
        load_owners.wait()
        for b in range(8):
            rows = slice(b * 128, b * 128 + 128)
            g = (groups_ref[b:b + 1, :] - c * 2).astype(F32)
            gmask[rows, :] = jnp.broadcast_to(g, (128, 128)).T
            o = (owners_ref[b:b + 1, :] - c * 2).astype(F32)
            omask[rows, :] = jnp.broadcast_to(o, (128, 128)).T

    def prepare_tcol():
        wait_bytes(tsq_recv.at[pl.ds(0, 7)], small_recv.at[0])
        total = tsq_recv[0]
        for k in range(1, 8):
            total = total + tsq_recv[k]
        for b in range(8):
            tcol[b * 128:b * 128 + 128, :] = jnp.broadcast_to(total[b:b + 1, :], (128, 128)).T

    load_coef.wait()
    for b, value in enumerate(blocks(coef)):
        set_weights(b, value)

    def first_compute(i, chunk):
        load_dos[i].wait()
        if i < 2:
            load_dos[i + 2].start()
        if i == 2:
            load_traits.start()
        if i == 3:
            load_tested.start()
            load_groups.start()
            load_owners.start()
        high, low = split(dos[pl.ds(pl.multiple_of(chunk * 256, 256), 256), :])
        ds[chunk, 0:256, :] = high
        ds[chunk, 256:512, :] = low
        value = chunk_dot(ds, chunk, weights[:, 0:256])
        if i == 0:
            pl.semaphore_wait(bar, 11)
        return value

    def plain_compute(i, chunk):
        return chunk_dot(ds, chunk, weights[:, 0:256])

    lane = lax.broadcasted_iota(jnp.int32, (1, K), 1)

    for it in range(ITERS):
        def residual_done(u, total):
            if it == 0 and u == 0:
                load_traits.wait()
            rows = piece(q, u, core)
            rfull[it, rows, :] = traits[rows, :] - total
            chrom_ag_send(it, rfull.at[it], u)

        chrom_rs(2 * it, first_compute if it == 0 else plain_compute, residual_done,
                 prepare_transposed if it == 0 else None)
        seen = []

        def use_residual(chunk):
            rows = rows256(chunk)
            high, low = split(rfull[it, rows, :])
            weights[rows, 0:K] = high
            weights[rows, K:2 * K] = low
            seen.append(rows)
            if len(seen) < 4:
                for v in range(4):
                    value = part_dot(dts, v, rows)
                    acc[v, :, 0:K] = value if len(seen) == 1 else acc[v, :, 0:K] + value

        chrom_ag_wait(it, rfull.at[it], use_residual)
        if it == 0:
            greeted(1)

        squares = []

        def gradient_done(u, total):
            grad = total * (1.0 / N)
            squares.append(jnp.sum(grad * grad, axis=0, keepdims=True))
            gfull[it, srows(s, u), :] = grad
            samp_ag_send(it, gfull.at[it, srows(s, u)], gfull.at[it, srows(s, u)], u)

        samp_rs(it, lambda v: acc[v, :, 0:K] + part_dot(dts, v, seen[3]), gradient_done)
        for u in range(4):
            for w in range(u * PARTS // 4, (u + 1) * PARTS // 4):
                samp_ag_wait(it, w)
            for b in (2 * u, 2 * u + 1):
                set_weights(b, gfull[it, b * 128:b * 128 + 128, :])
            if u < 3:
                for v in range(4):
                    value = part_dot(ds, v, slice(u * 256, u * 256 + 256))
                    acc[v, :, 0:K] = value if u == 0 else acc[v, :, 0:K] + value
        g_row = sum(squares[1:], squares[0])
        g_row = g_row + pltpu.roll(g_row, 64, 1)
        image_squares = []
        chrom_rs(2 * it + 1, lambda i, chunk: acc[chunk, :, 0:K] + part_dot(ds, chunk, slice(768, 1024)),
                 lambda u, total: image_squares.append(jnp.sum(total * total, axis=0, keepdims=True)),
                 prepare_tsq if it == 0 else None)
        i_row = sum(image_squares[1:], image_squares[0])
        i_row = i_row + pltpu.roll(i_row, 64, 1)
        scal[it, pl.ds(me, 1), :] = jnp.where(lane < 64, g_row, i_row)

        for far_s, far_c in everyone:
            remote(scal.at[it, pl.ds(me, 1)], scal.at[it, pl.ds(me, 1)], scal_send.at[it], scal_recv.at[it],
                   (far_s, far_c)).start()
        for work in ((prepare_tested,), (prepare_masks, prepare_tcol))[it]:
            work()
        wait_bytes(scal.at[it, pl.ds(0, 127)], scal_recv.at[it])
        sums = jnp.sum(scal[it], axis=0, keepdims=True)
        grad_sq = jnp.sum(jnp.where(lane < 64, sums, 0.0), axis=1, keepdims=True)
        image_sq = jnp.sum(jnp.where(lane < 64, 0.0, sums), axis=1, keepdims=True)
        step = grad_sq / (image_sq * (1.0 / N) + 1e-06)
        limit = step * PENALTY
        for b in range(8):
            rows = slice(b * 128, b * 128 + 128)
            moved = coef[rows, :] + step * gfull[it, rows, :]
            length = jnp.sqrt(jnp.sum(moved * moved, axis=1, keepdims=True))
            new = moved * (jnp.maximum(length - limit, 0.0) / jnp.maximum(length, limit))
            coef[rows, :] = new
            set_weights(b, new)

    def own_parts():
        for b in range(8):
            set_weights(b, coef[b * 128:b * 128 + 128, :] * (1.0 - gmask[b * 128:b * 128 + 128, :]), 256)
        for i, chunk in enumerate(order):
            rows = rows256(chunk)
            value = chunk_dot(ds, chunk, weights[:, 256:512])
            own0[rows, :] = value
            own1[rows, :] = part[4, i] - value

    def last_residual_done(u, total):
        rows = piece(q, u, core)
        rfull[2, rows, :] = traits[rows, :] - total
        chrom_ag_send(2, rfull.at[2], u)

    chrom_rs(4, plain_compute, last_residual_done, own_parts)
    sq = []
    seen_last = []

    def use_last(chunk):
        rows = rows256(chunk)
        res = rfull[2, rows, :]
        loco0 = res + own0[rows, :]
        loco1 = res + own1[rows, :]
        sq.append((jnp.sum(loco0 * loco0, axis=0, keepdims=True), jnp.sum(loco1 * loco1, axis=0, keepdims=True)))
        loco_w[rows, 0:K] = loco0.astype(BF16)
        loco_w[rows, K:2 * K] = loco1.astype(BF16)
        seen_last.append(rows)
        if len(seen_last) < 4:
            for v in range(4):
                value = products_of(v, rows)
                acc[v] = value if len(seen_last) == 1 else acc[v] + value

    def products_of(v, depth):
        return jnp.dot(tts[v, :, depth], loco_w[depth, :], preferred_element_type=F32)

    chrom_ag_wait(2, rfull.at[2], use_last)
    give_resid = pltpu.make_async_copy(rfull.at[2], resid_out, out_sem.at[0])
    give_resid.start()

    def products(v):
        out = acc[v] + products_of(v, seen_last[3])
        return jnp.where(omask[v * 256:v * 256 + 256, :] < 0.5, out[:, :K], out[:, K:])

    def send_squares():
        lsq_recv[s, 0:1, :] = (sq[0][0] + sq[1][0]) + (sq[2][0] + sq[3][0])
        lsq_recv[s, 1:2, :] = (sq[0][1] + sq[1][1]) + (sq[2][1] + sq[3][1])
        for k in samp_order:
            remote(lsq_recv.at[s], lsq_recv.at[s], small_send.at[1], small_recv.at[1], (samp_peer(k), c)).start()

    def score_done(u, picked):
        if u == 0:
            wait_bytes(lsq_recv.at[pl.ds(0, 7)], small_recv.at[1])
        lsum = lsq_recv[0]
        for k in range(1, 8):
            lsum = lsum + lsq_recv[k]
        rows = srows(s, u)
        lpick = jnp.where(omask[rows, :] < 0.5, lsum[0:1, :], lsum[1:2, :])
        denom = math.sqrt(N) * jnp.sqrt((tcol[rows, :] * (1.0 / N) + 1e-06) * (lpick * (1.0 / N) + 1e-06))
        score[u] = picked / denom
        samp_ag_send(2, score.at[u], scores_out.at[rows], u)
        pltpu.make_async_copy(score.at[u], scores_out.at[rows], out_sem.at[1 + u]).start()

    send_squares()
    samp_rs(2, products, score_done)
    for u in range(PARTS):
        samp_ag_wait(2, u)
        wait_bytes(score.at[u], out_sem.at[1 + u])
    give_resid.wait()

    for ph in range(5):
        for u in range(2):
            wait_bytes(corebuf.at[ph, u], core_send.at[ph, u])
        wait_bytes(rfull.at[0, pl.ds(0, 448)], crs_send.at[ph])
    for a in range(3):
        wait_bytes(rfull.at[0, pl.ds(0, 448)], cag_send.at[a])
        wait_bytes(rfull.at[0, pl.ds(0, 512)], fwd_send.at[a])
        wait_bytes(rfull.at[0, pl.ds(0, 896)], srs_send.at[a])
        wait_bytes(rfull.at[0, pl.ds(0, 896)], sag_send.at[a])
    for it in range(ITERS):
        wait_bytes(scal.at[it, pl.ds(0, 127)], scal_send.at[it])
    wait_bytes(tsq_recv.at[pl.ds(0, 7)], small_send.at[0])
    wait_bytes(lsq_recv.at[pl.ds(0, 7)], small_send.at[1])


def hand_over_kernel(a_in, b_in, a_out, b_out, buf, in_sem, out_sem):
    pairs = [(a_in, a_out, i) for i in range(2)] + [(b_in, b_out, i) for i in range(2)]
    loads, stores = [], []
    for n, (src, _, i) in enumerate(pairs):
        loads.append(pltpu.make_async_copy(src.at[pl.ds(i * 512, 512)], buf.at[n], in_sem.at[n]))
        loads[-1].start()
    for n, (_, dst, i) in enumerate(pairs):
        loads[n].wait()
        stores.append(pltpu.make_async_copy(buf.at[n], dst.at[pl.ds(i * 512, 512)], out_sem.at[n]))
        stores[-1].start()
    for cp in stores:
        cp.wait()


def body(dosages, traits, start_coef, groups, tested, owners):
    any_spec = pl.BlockSpec(memory_space=pl.ANY)
    V = pltpu.VMEM
    DMA = pltpu.SemaphoreType.DMA
    out = jax.ShapeDtypeStruct((ROWS, K), F32)
    scores, resid = pl.pallas_call(
        kernel,
        out_shape=(out, out),
        in_specs=[any_spec] * 6,
        out_specs=(any_spec, any_spec),
        scratch_shapes=[
            V((8, K), jnp.int32), V((8, K), jnp.int32),
            V((1024, 1024), F32), V((1024, K), F32), V((1024, K), F32), V((1024, 1024), BF16),
            V((4, 512, 1024), BF16), V((4, 512, 1024), BF16), V((4, 256, 1024), BF16),
            V((1024, 512), BF16), V((1024, 256), BF16),
            V((5, 4, 256, K), F32), V((5, 512, K), F32), V((5, 2, 256, K), F32), V((5, PIECES, 8, PIECE, K), F32),
            V((3, 1024, K), F32), V((3, 1024, K), F32), V((3, PARTS, 8, PART, K), F32), V((2, 1024, K), F32),
            V((PARTS, PART, K), F32), V((4, 256, 2 * K), F32),
            V((1024, K), F32), V((1024, K), F32), V((1024, K), F32), V((1024, K), F32), V((1024, K), F32),
            V((8, 8, K), F32), V((8, 2, K), F32), V((2, 128, K), F32),
            DMA((9,)), DMA((5, 2)), DMA((5, 2)), DMA((5,)), DMA((5, PIECES)), DMA((3,)), DMA((3, PIECES, 8)),
            DMA((3,)), DMA((3, PIECES)), DMA((3,)), DMA((3, PARTS)), DMA((3,)), DMA((3, PARTS)),
            DMA((2,)), DMA((2,)), DMA((2,)), DMA((2,)), DMA((1 + PARTS,)), pltpu.SemaphoreType.REGULAR((2,)),
        ],
        compiler_params=pltpu.CompilerParams(
            collective_id=0, has_side_effects=True, vmem_limit_bytes=62 * 1024 * 1024
        ),
    )(dosages, traits, start_coef, groups.reshape(8, 128), tested, owners.reshape(8, 128))
    return pl.pallas_call(
        hand_over_kernel,
        out_shape=(out, out),
        in_specs=[any_spec, any_spec],
        out_specs=(any_spec, any_spec),
        scratch_shapes=[V((4, 512, K), F32), DMA((4,)), DMA((4,))],
    )(scores, resid)


def solution(mesh):
    placed = (P("samp", "chrom"), P("samp", None), P("chrom", None), P("chrom"), P("samp", "chrom"), P("chrom"))
    return jax.shard_map(
        body, mesh=mesh, in_specs=placed, out_specs=(P("chrom", None), P("samp", None)), check_vma=False
    )
```
